32 devices in a mesh: seq: 4 (over z), mp: 8 (over y, x, core).
Axes of the slice: x: 2, y: 2, z: 4, core: 2. Of those that a mesh axis runs over, the one named last changes fastest.
Arguments:
- enc_rows: bfloat16 [1024, 1024], P('seq', 'mp'), may hold values from -6 to 6
- ffn_in: bfloat16 [1024, 65536], P('seq', 'mp'), may hold values from -0.1875 to 0.1875
- ffn_out: bfloat16 [65536, 1024], P('mp', 'seq'), may hold values from -0.03125 to 0.03125
- enc_gain: float32 [1024], replicated, may hold values from 0.25 to 1.75
- final_gain: float32 [1024], replicated, may hold values from 0.25 to 1.75
- sent_lengths: int32 [4, 4], replicated, may hold values from 1 to 128, 256 in all within a row
- group_table: int32 [4, 4], replicated, may hold values from 0 to 3, as said below
- dec_rows: bfloat16 [1024, 1024], P('seq', 'mp'), may hold values from -6 to 6
- dec_gain: float32 [2, 1024], replicated, may hold values from 0.25 to 1.75
- w_query: bfloat16 [2, 1024, 8192], P(None, None, 'mp'), may hold values from -0.1875 to 0.1875
- w_key: bfloat16 [2, 1024, 8192], P(None, None, 'mp'), may hold values from -0.1875 to 0.1875
- w_value: bfloat16 [2, 1024, 8192], P(None, None, 'mp'), may hold values from -0.1875 to 0.1875
- w_output: bfloat16 [2, 8192, 1024], P(None, 'mp'), may hold values from -0.0625 to 0.0625
Outputs:
- dec_out: bfloat16 [1024, 1024], P('seq', 'mp')
The draws below stay inside these ranges and needn't reach their ends.
Inputs may be any that keep to these rules, and one draw needn't show every extreme that they name: `sent_lengths`: each row sums to 256; each row has an entry equal to 128. `group_table`: every row and every column holds each group number exactly once.
All inputs are finite; a program needn't handle non-finite values.
Results may differ from the reference program's by a relative error of at most 0.014.
Values may be sent and summed in bfloat16 or wider, within the bound.
A program may use at most 128 MiB of HBM per device.

```python
import math
import jax
import jax.numpy as jnp
import numpy as np
from jax import lax

D = 1024
FF = 65536
DH = 128
HEADS = 64
LAYERS = 2
ROWS_DEV = 256
TGT_GRP = 256
ENC_ROWS = 1024
SENT_DEV = 4
MAXLEN = 128
TGT_ALL = 1024
HD = 8192
N_SEQ = 4


def draw_group_table(key, part):
    row_perm = jax.random.permutation(jax.random.fold_in(key, 11), N_SEQ)
    col_perm = jax.random.permutation(jax.random.fold_in(key, 12), N_SEQ)
    return ((row_perm[:, None] + col_perm[None, :]) % N_SEQ).astype(jnp.int32)


def draw_w_query(key, part):
    full_shape = (LAYERS, D, HEADS * DH)
    return (jnp.clip(jax.random.normal(key, full_shape, jnp.float32), -6.0, 6.0) * D ** (-0.5)).astype(jnp.bfloat16)


def levels(key, extent, cuts, least, high):
    level, own = 1.0, jax.random.fold_in(key, 6)
    for dim, parts in cuts:
        steps = jnp.exp(jax.random.uniform(jax.random.fold_in(own, dim), (parts,), jnp.float32, least / len(cuts), high / len(cuts)))
        level = level * jnp.repeat(steps, extent[dim] // parts).reshape([-1 if axis == dim else 1 for axis in range(len(extent))])
    return level


def profile(amount, total, reach, skew):
    loads = [(1 << 20) // math.isqrt(standing ** skew) + 1 for standing in range(2, amount + 1)]
    spare, holding = total - reach - (amount - 1), [1] * (amount - 1)
    while spare > 0:
        candidates = [i for i in range(amount - 1) if holding[i] < reach]
        mass, remaining = sum([loads[i] for i in candidates]), spare
        for i in candidates:
            addition = min(reach - holding[i], max(1, remaining * loads[i] // mass), spare)
            holding[i] = holding[i] + addition
            spare = spare - addition
    return np.array([reach] + holding)


def uneven(stream_key, count, total, reach, lean):
    if count == 2:
        one = jax.random.randint(stream_key, (), max(1, total - reach), min(reach, total - 1) + 1)
        return jnp.stack([one, total - one])
    tallies = jnp.asarray(profile(count, total, reach, lean), jnp.int32)
    twos = (count - 1) // 2
    source_of, taker = tallies[1:1 + 2 * twos:2], tallies[2:2 + 2 * twos:2]
    slack = jnp.minimum(source_of - 1, reach - taker)
    shifted = jax.random.randint(jax.random.fold_in(stream_key, 1), (twos,), 0, 1 << 20) % (slack + 1)
    tallies = tallies.at[1:1 + 2 * twos:2].set(source_of - shifted).at[2:2 + 2 * twos:2].set(taker + shifted)
    return tallies[jax.random.permutation(jax.random.fold_in(stream_key, 2), count)]


def centred(own_key, shape, deviation, most, pieces=(), held_as=jnp.bfloat16):
    result = jax.random.normal(own_key, shape, jnp.float32) * deviation
    if len(pieces) > 0:
        result = levels(own_key, shape, pieces, -0.22, 0.18) * result
    return jnp.clip(result, min=-most, max=most).astype(held_as)


def setup_inputs(seed: int = 0) -> dict:
    splits = jax.random.split(jax.random.key(seed), 14)
    return {
        "enc_rows": centred(splits[0], (ENC_ROWS, D), 1.0, 6.0, ((0, 4), (1, 8))),
        "ffn_in": centred(splits[1], (D, FF), D ** -0.5, 0.1875, ((0, 4), (1, 8))),
        "ffn_out": centred(splits[2], (FF, D), (FF // 2) ** -0.5, 0.03125, ((0, 8), (1, 4))),
        "enc_gain": jnp.clip(1.0 + 0.15 * jax.random.normal(splits[3], (D,), jnp.float32), 0.25, 1.75),
        "final_gain": jnp.clip(1.0 + 0.15 * jax.random.normal(splits[4], (D,), jnp.float32), 0.25, 1.75),
        "sent_lengths": jax.vmap(lambda own: uneven(own, SENT_DEV, ROWS_DEV, MAXLEN, 2))(jax.random.split(splits[5], N_SEQ)).reshape((N_SEQ, SENT_DEV)).astype(jnp.int32),
        "group_table": draw_group_table(jax.random.fold_in(splits[13], 71), 0),
        "dec_rows": centred(splits[7], (TGT_ALL, D), 1.0, 6.0, ((0, 4), (1, 8))),
        "dec_gain": jnp.clip(1.0 + 0.15 * jax.random.normal(splits[8], (LAYERS, D), jnp.float32), 0.25, 1.75),
        "w_query": draw_w_query(jax.random.fold_in(splits[13], 71), 0),
        "w_key": centred(splits[10], (LAYERS, D, HD), D ** -0.5, 0.1875, ((2, 8),)),
        "w_value": centred(splits[11], (LAYERS, D, HD), D ** -0.5, 0.1875, ((2, 8),)),
        "w_output": centred(splits[12], (LAYERS, HD, D), HD ** -0.5, 0.0625, ((1, 8),)),
    }


epsilon = 1e-06

def rms_scale(values, gain_row):
    mean_square = lax.optimization_barrier(jnp.mean(values * values, axis=-1, keepdims=True))
    return values * lax.rsqrt(mean_square + epsilon) * gain_row

def reference(enc_rows, ffn_in, ffn_out, enc_gain, final_gain, sent_lengths, group_table, dec_rows, dec_gain, w_query, w_key, w_value, w_output):

    def encode_block(block_rows):
        block_float = block_rows.astype(jnp.float32)
        normed = rms_scale(block_float, enc_gain).astype(jnp.bfloat16)
        hidden = jnp.maximum(jnp.dot(normed, ffn_in, preferred_element_type=jnp.float32), 0.0).astype(jnp.bfloat16)
        encoded = block_float + jnp.dot(hidden, ffn_out, preferred_element_type=jnp.float32)
        return rms_scale(encoded, final_gain).astype(jnp.bfloat16)
    memory = lax.map(encode_block, enc_rows.reshape(N_SEQ, ROWS_DEV, D)).reshape(N_SEQ * ROWS_DEV, D)
    group_ids = jnp.arange(N_SEQ, dtype=jnp.int32)
    starts = (jnp.cumsum(sent_lengths, axis=1) - sent_lengths).astype(jnp.int32)
    matches = group_table[None, :, :] == group_ids[:, None, None]
    chosen_len = lax.optimization_barrier(jnp.sum(jnp.where(matches, sent_lengths[None], 0), axis=2)).astype(jnp.int32)
    chosen_start = lax.optimization_barrier(jnp.sum(jnp.where(matches, starts[None], 0), axis=2)).astype(jnp.int32)
    positions = jnp.arange(MAXLEN, dtype=jnp.int32)
    row_index = (group_ids[None, :, None] * ROWS_DEV + jnp.minimum(chosen_start[:, :, None] + positions[None, None, :], ROWS_DEV - 1)).astype(jnp.int32)
    padded_memory = memory[row_index]
    live_mask = positions[None, None, :] < chosen_len[:, :, None]
    states = dec_rows.astype(jnp.float32).reshape(N_SEQ, N_SEQ, TGT_GRP // N_SEQ, D)

    def decode_group(inputs):
        group_memory, group_mask, state = inputs
        q_rows = state.shape[1]
        for layer_index in range(LAYERS):
            state_half = lax.optimization_barrier(state.astype(jnp.bfloat16))
            normed = rms_scale(state_half.astype(jnp.float32), dec_gain[layer_index]).astype(jnp.bfloat16)
            queries = (jnp.dot(normed, w_query[layer_index], preferred_element_type=jnp.float32) * DH ** (-0.5)).astype(jnp.bfloat16)
            key_rows = jnp.dot(group_memory, w_key[layer_index], preferred_element_type=jnp.float32).astype(jnp.bfloat16)
            value_rows = jnp.dot(group_memory, w_value[layer_index], preferred_element_type=jnp.float32).astype(jnp.bfloat16)
            queries, key_rows, value_rows = lax.optimization_barrier((queries, key_rows, value_rows))
            query_heads = queries.reshape(N_SEQ, q_rows, HEADS, DH).astype(jnp.float32)
            key_heads = key_rows.reshape(N_SEQ, MAXLEN, HEADS, DH).astype(jnp.float32)
            value_heads = value_rows.reshape(N_SEQ, MAXLEN, HEADS, DH).astype(jnp.float32)
            scores = jnp.einsum('sqhd,sthd->shqt', query_heads, key_heads)
            scores = jnp.where(group_mask[:, None, None, :], scores, -jnp.inf)
            weights = lax.optimization_barrier(jax.nn.softmax(scores, axis=-1).astype(jnp.bfloat16))
            attended = jnp.einsum('shqt,sthd->sqhd', weights.astype(jnp.float32), value_heads).astype(jnp.bfloat16)
            attended = attended.reshape(N_SEQ, q_rows, HEADS * DH)
            state = state + jnp.dot(attended, w_output[layer_index], preferred_element_type=jnp.float32)
        return state.astype(jnp.bfloat16)
    outputs = lax.map(decode_group, (padded_memory, live_mask, states))
    return outputs.reshape(N_SEQ * TGT_GRP, D)
```

```python
import functools

import jax
import jax.numpy as jnp
from jax import lax
from jax.experimental import pallas as pl
from jax.experimental.pallas import tpu as pltpu
from jax.sharding import PartitionSpec as P

MESH = pl.DeviceIdType.MESH

D = 1024
DH = 128
LAYERS = 2


epsilon = 1e-06


def rms_scale(values, gain_row):
    mean_square = jnp.mean(values * values, axis=-1, keepdims=True)
    return values * lax.rsqrt(mean_square + epsilon) * gain_row


def flip(index, bits):
    out = index
    for power in (1, 2, 4, 8, 16, 32):
        if bits & power:
            out = out + power - 2 * power * ((out // power) % 2)
    return out


def z_order(count):
    return sorted(range(1, count), key=lambda bits: (bits == 1, bits))


def ffn_kernel(
    n_seq,
    n_mp,
    enc_ref,
    gain_ref,
    fin_ref,
    fout_ref,
    share_ref,
    enc_all,
    normed,
    win,
    wout,
    hidden,
    part_out,
    part_in,
    z_out,
    z_in,
    enc_zs,
    enc_zr,
    enc_ps,
    enc_pr,
    in_s,
    in_r,
    out_s,
    out_r,
    red_ps,
    red_pr,
    red_zs,
    red_zr,
    local_sem,
):
    s = lax.axis_index("seq")
    m = lax.axis_index("mp")
    rows, width = enc_ref.shape
    depth = fin_ref.shape[0]
    units = fin_ref.shape[1] // n_seq
    out_width = fout_ref.shape[1]
    total_rows = rows * n_seq
    per_block = out_width // width

    barrier = pltpu.get_barrier_semaphore()
    for bits in range(1, n_seq):
        pl.semaphore_signal(barrier, inc=1, device_id=(flip(s, bits), m), device_id_type=MESH)
    for bits in range(1, n_mp):
        pl.semaphore_signal(barrier, inc=1, device_id=(s, flip(m, bits)), device_id_type=MESH)
    pl.semaphore_wait(barrier, n_seq + n_mp - 2)

    my_rows = pl.ds(pl.multiple_of(s * rows, rows), rows)

    own_enc = pltpu.make_async_copy(enc_ref, enc_all.at[m, my_rows], local_sem.at[0])
    own_enc.start()
    enc_z = []
    for bits in z_order(n_seq):
        copy = pltpu.make_async_remote_copy(
            src_ref=enc_ref,
            dst_ref=enc_all.at[m, my_rows],
            send_sem=enc_zs.at[bits],
            recv_sem=enc_zr.at[bits],
            device_id=(flip(s, bits), m),
            device_id_type=MESH,
        )
        copy.start()
        enc_z.append(copy)

    own_in = pltpu.make_async_copy(
        fin_ref.at[:, pl.ds(pl.multiple_of(s * units, units), units)], win.at[s], local_sem.at[1]
    )
    own_in.start()
    own_out = pltpu.make_async_copy(
        fout_ref.at[pl.ds(pl.multiple_of(s * units, units), units)], wout.at[s], local_sem.at[2]
    )
    own_out.start()
    in_copies = []
    out_copies = []
    for bits in z_order(n_seq):
        peer = flip(s, bits)
        copy = pltpu.make_async_remote_copy(
            src_ref=fin_ref.at[:, pl.ds(pl.multiple_of(peer * units, units), units)],
            dst_ref=win.at[s],
            send_sem=in_s.at[bits],
            recv_sem=in_r.at[bits],
            device_id=(peer, m),
            device_id_type=MESH,
        )
        copy.start()
        in_copies.append(copy)
    for bits in z_order(n_seq):
        peer = flip(s, bits)
        copy = pltpu.make_async_remote_copy(
            src_ref=fout_ref.at[pl.ds(pl.multiple_of(peer * units, units), units)],
            dst_ref=wout.at[s],
            send_sem=out_s.at[bits],
            recv_sem=out_r.at[bits],
            device_id=(peer, m),
            device_id_type=MESH,
        )
        copy.start()
        out_copies.append(copy)

    own_enc.wait()
    for copy in enc_z:
        copy.wait()

    enc_p = []
    for bits in range(1, n_mp):
        copy = pltpu.make_async_remote_copy(
            src_ref=enc_all.at[m],
            dst_ref=enc_all.at[m],
            send_sem=enc_ps.at[bits],
            recv_sem=enc_pr.at[bits],
            device_id=(s, flip(m, bits)),
            device_id_type=MESH,
        )
        copy.start()
        enc_p.append(copy)
    for copy in enc_p:
        copy.wait()

    chunk = min(256, rows)

    def norm_chunk(i, carry):
        span = pl.ds(pl.multiple_of(i * chunk, chunk), chunk)
        squares = jnp.zeros((chunk, 1), jnp.float32)
        for k in range(n_mp):
            value = enc_all[k, span, :].astype(jnp.float32)
            squares = squares + jnp.sum(value * value, axis=1, keepdims=True)
        scale = lax.rsqrt(squares / (n_mp * width) + epsilon)
        for k in range(n_mp):
            cols = pl.ds(k * width, width)
            value = enc_all[k, span, :].astype(jnp.float32)
            normed[span, cols] = (value * scale * gain_ref[:, cols]).astype(jnp.bfloat16)
        return carry

    lax.fori_loop(0, total_rows // chunk, norm_chunk, 0)

    own_in.wait()
    for copy in in_copies:
        copy.wait()

    tile = min(256, units)

    def hidden_chunk(i, carry):
        cols = pl.ds(pl.multiple_of((i % (units // tile)) * tile, tile), tile)
        span = pl.ds(pl.multiple_of((i // (units // tile)) * chunk, chunk), chunk)
        acc = jnp.zeros((chunk, tile), jnp.float32)
        for k in range(n_seq):
            acc = acc + jnp.dot(
                normed[span, pl.ds(k * depth, depth)],
                win[k, :, cols],
                preferred_element_type=jnp.float32,
            )
        hidden[span, cols] = jnp.maximum(acc, 0.0).astype(jnp.bfloat16)
        return carry

    lax.fori_loop(0, (total_rows // chunk) * (units // tile), hidden_chunk, 0)

    own_out.wait()

    def out_block(block):
        def rows_chunk(i, carry):
            span = pl.ds(pl.multiple_of(i * chunk, chunk), chunk)
            value = jnp.dot(hidden[span, :], wout[block], preferred_element_type=jnp.float32)
            for j in range(per_block):
                part_out[block * per_block + j, span, :] = value[
                    :, j * width : (j + 1) * width
                ].astype(jnp.bfloat16)
            return carry

        lax.fori_loop(0, total_rows // chunk, rows_chunk, 0)

    def send_copy(slot):
        return pltpu.make_async_remote_copy(
            src_ref=part_out.at[slot],
            dst_ref=part_in.at[m],
            send_sem=red_ps.at[slot],
            recv_sem=red_pr.at[m],
            device_id=(s, slot),
            device_id_type=MESH,
        )

    def send_block(block):
        out_block(block)
        for j in range(per_block):
            slot = block * per_block + j

            @pl.when(slot != m)
            def _():
                send_copy(slot).start()

    send_block(s)
    for bits, copy in zip(z_order(n_seq), out_copies):
        copy.wait()
        send_block(flip(s, bits))

    for bits in range(1, n_mp):
        send_copy(flip(m, bits)).wait_send()
    for bits in range(1, n_mp):
        peer = flip(m, bits)
        pltpu.make_async_remote_copy(
            src_ref=part_out.at[peer],
            dst_ref=part_in.at[peer],
            send_sem=red_ps.at[peer],
            recv_sem=red_pr.at[peer],
            device_id=(s, peer),
            device_id_type=MESH,
        ).wait_recv()

    def reduce_rows(block):
        span = pl.ds(pl.multiple_of(block * rows, rows), rows)
        total = part_out[m, span, :].astype(jnp.float32)
        for bits in range(1, n_mp):
            total = total + part_in[flip(m, bits), span, :].astype(jnp.float32)
        return total

    red_z = []
    for bits in z_order(n_seq):
        peer = flip(s, bits)
        z_out[bits] = reduce_rows(peer).astype(jnp.bfloat16)
        copy = pltpu.make_async_remote_copy(
            src_ref=z_out.at[bits],
            dst_ref=z_in.at[bits],
            send_sem=red_zs.at[bits],
            recv_sem=red_zr.at[bits],
            device_id=(peer, m),
            device_id_type=MESH,
        )
        copy.start()
        red_z.append(copy)
    total = reduce_rows(s)
    for bits, copy in zip(z_order(n_seq), red_z):
        copy.wait()
        total = total + z_in[bits].astype(jnp.float32)
    share_ref[...] = enc_ref[...].astype(jnp.float32) + total


def ffn_fast(enc_rows, ffn_in, ffn_out, enc_gain):
    n_seq, n_mp = lax.axis_size("seq"), lax.axis_size("mp")
    rows, width = enc_rows.shape
    depth, units = ffn_in.shape[0], ffn_in.shape[1] // n_seq
    out_width = ffn_out.shape[1]
    total = rows * n_seq
    full = width * n_mp
    dma = pltpu.SemaphoreType.DMA
    return pl.pallas_call(
        functools.partial(ffn_kernel, n_seq, n_mp),
        out_shape=jax.ShapeDtypeStruct((rows, width), jnp.float32),
        in_specs=[
            pl.BlockSpec(memory_space=pltpu.VMEM),
            pl.BlockSpec(memory_space=pltpu.VMEM),
            pl.BlockSpec(memory_space=pl.ANY),
            pl.BlockSpec(memory_space=pl.ANY),
        ],
        out_specs=pl.BlockSpec(memory_space=pltpu.VMEM),
        scratch_shapes=[
            pltpu.VMEM((n_mp, total, width), jnp.bfloat16),
            pltpu.VMEM((total, full), jnp.bfloat16),
            pltpu.VMEM((n_seq, depth, units), jnp.bfloat16),
            pltpu.VMEM((n_seq, units, out_width), jnp.bfloat16),
            pltpu.VMEM((total, units), jnp.bfloat16),
            pltpu.VMEM((n_mp, total, width), jnp.bfloat16),
            pltpu.VMEM((n_mp, total, width), jnp.bfloat16),
            pltpu.VMEM((n_seq, rows, width), jnp.bfloat16),
            pltpu.VMEM((n_seq, rows, width), jnp.bfloat16),
            dma((n_seq,)),
            dma((n_seq,)),
            dma((n_mp,)),
            dma((n_mp,)),
            dma((n_seq,)),
            dma((n_seq,)),
            dma((n_seq,)),
            dma((n_seq,)),
            dma((n_mp,)),
            dma((n_mp,)),
            dma((n_seq,)),
            dma((n_seq,)),
            dma((3,)),
        ],
        compiler_params=pltpu.CompilerParams(
            collective_id=0, has_side_effects=True, vmem_limit_bytes=48 * 1024 * 1024
        ),
    )(enc_rows, enc_gain.reshape(1, full), ffn_in, ffn_out)


def fast_shapes(enc_rows, ffn_in, ffn_out):
    n_seq, n_mp = lax.axis_size("seq"), lax.axis_size("mp")
    power = (n_seq & (n_seq - 1)) == 0 and (n_mp & (n_mp - 1)) == 0
    aligned = (
        enc_rows.shape[1] % 128 == 0
        and ffn_in.shape[0] % 128 == 0
        and (ffn_in.shape[1] // n_seq) % 256 == 0
        and ffn_out.shape[1] % enc_rows.shape[1] == 0
        and enc_rows.shape[0] % 256 == 0
    )
    return power and aligned


def shards(
    enc_rows,
    ffn_in,
    ffn_out,
    enc_gain,
    final_gain,
    sent_lengths,
    group_table,
    dec_rows,
    dec_gain,
    w_query,
    w_key,
    w_value,
    w_output,
):
    group_count = lax.axis_size("seq")
    my_group = lax.axis_index("seq")
    col_width = enc_rows.shape[1]
    col_start = lax.axis_index("mp") * col_width
    row_count = enc_rows.shape[0]
    max_length = 2 * row_count // group_count
    fast = fast_shapes(enc_rows, ffn_in, ffn_out)
    if fast:
        encoded = ffn_fast(enc_rows, ffn_in, ffn_out, enc_gain)
    else:
        whole_rows = lax.all_gather(enc_rows, "mp", axis=1, tiled=True)
        normed = rms_scale(whole_rows.astype(jnp.float32), enc_gain).astype(jnp.bfloat16)
        full_in = lax.all_gather(ffn_in, "seq", axis=0, tiled=True)
        inner = jnp.dot(normed, full_in, preferred_element_type=jnp.float32)
        hidden = jnp.maximum(inner, 0.0).astype(jnp.bfloat16)
        partial_out = jnp.dot(
            hidden,
            lax.all_gather(ffn_out, "seq", axis=1, tiled=True),
            preferred_element_type=jnp.float32,
        )
    my_lengths = lax.dynamic_index_in_dim(sent_lengths, my_group, 0, keepdims=False)
    my_targets = lax.dynamic_index_in_dim(group_table, my_group, 0, keepdims=False)
    my_starts = jnp.cumsum(my_lengths) - my_lengths
    group_ids = jnp.arange(group_count, dtype=jnp.int32)
    matches = my_targets[None, :] == group_ids[:, None]
    send_starts = jnp.sum(jnp.where(matches, my_starts[None, :], 0), axis=1)
    positions = jnp.arange(max_length, dtype=jnp.int32)
    row_index = jnp.minimum(send_starts[:, None] + positions[None, :], row_count - 1)
    recv_lengths = jnp.sum(jnp.where(group_table == my_group, sent_lengths, 0), axis=1)
    live_mask = positions[None, :] < recv_lengths[:, None]
    kv_width = w_key.shape[2]
    weight_list = []
    for layer_index in range(LAYERS):
        weight_list.append(w_key[layer_index])
        weight_list.append(w_value[layer_index])
    if not fast:
        enc_share = lax.psum_scatter(partial_out, "mp", scatter_dimension=1, tiled=True)
        encoded = enc_rows.astype(jnp.float32) + enc_share
    squares = lax.psum(jnp.sum(encoded * encoded, axis=1), "mp")
    gain_part = lax.dynamic_slice_in_dim(final_gain, col_start, col_width, 0)
    memory = (encoded * lax.rsqrt(squares / D + epsilon)[:, None] * gain_part).astype(jnp.bfloat16)
    blocks = memory[row_index]
    gathered = lax.all_gather(
        lax.all_to_all(blocks, "seq", split_axis=0, concat_axis=0, tiled=True),
        "mp",
        axis=2,
        tiled=True,
    )
    projected = tuple(
        (
            jnp.einsum(
                "std,de->ste", gathered, weight_matrix, preferred_element_type=jnp.float32
            ).astype(jnp.bfloat16)
            for weight_matrix in weight_list
        )
    )
    tgt_rows = dec_rows.shape[0]
    per_sentence = tgt_rows // group_count
    local_heads = kv_width // DH
    final_state = dec_rows.astype(jnp.float32)
    for layer_index in range(LAYERS):
        state_half = lax.all_gather(final_state.astype(jnp.bfloat16), "mp", axis=1, tiled=True)
        normed_rows = rms_scale(state_half.astype(jnp.float32), dec_gain[layer_index]).astype(
            jnp.bfloat16
        )
        queries = (
            jnp.dot(normed_rows, w_query[layer_index], preferred_element_type=jnp.float32)
            * DH ** (-0.5)
        ).astype(jnp.bfloat16)
        query_heads = queries.reshape(group_count, per_sentence, local_heads, DH)
        key_heads = projected[2 * layer_index].reshape(group_count, max_length, local_heads, DH)
        value_heads = projected[2 * layer_index + 1].reshape(
            group_count, max_length, local_heads, DH
        )
        scores = jnp.einsum(
            "sqhd,sthd->shqt", query_heads, key_heads, preferred_element_type=jnp.float32
        )
        scores = jnp.where(live_mask[:, None, None, :], scores, -jnp.inf)
        weights = jax.nn.softmax(scores, axis=-1).astype(jnp.bfloat16)
        attended = jnp.einsum(
            "shqt,sthd->sqhd", weights, value_heads, preferred_element_type=jnp.float32
        ).astype(jnp.bfloat16)
        final_state = final_state + lax.psum_scatter(
            jnp.dot(
                attended.reshape(tgt_rows, kv_width),
                w_output[layer_index],
                preferred_element_type=jnp.float32,
            ).astype(jnp.bfloat16),
            "mp",
            scatter_dimension=1,
            tiled=True,
        ).astype(jnp.float32)
    return final_state.astype(jnp.bfloat16)


def solution(mesh):
    in_specs = (
        P("seq", "mp"),
        P("seq", "mp"),
        P("mp", "seq"),
        P(),
        P(),
        P(),
        P(),
        P("seq", "mp"),
        P(),
        P(None, None, "mp"),
        P(None, None, "mp"),
        P(None, None, "mp"),
        P(None, "mp", None),
    )
    out_specs = P("seq", "mp")
    return jax.shard_map(shards, mesh=mesh, in_specs=in_specs, out_specs=out_specs, check_vma=False)
```

```python
import functools

import jax
import jax.numpy as jnp
from jax import lax
from jax.experimental import pallas as pl
from jax.experimental.pallas import tpu as pltpu
from jax.sharding import PartitionSpec as P

MESH = pl.DeviceIdType.MESH

D = 1024
DH = 128
LAYERS = 2


epsilon = 1e-06


def rms_scale(values, gain_row):
    mean_square = jnp.mean(values * values, axis=-1, keepdims=True)
    return values * lax.rsqrt(mean_square + epsilon) * gain_row


def flip(index, bits):
    out = index
    for power in (1, 2, 4, 8, 16, 32):
        if bits & power:
            out = out + power - 2 * power * ((out // power) % 2)
    return out


def z_order(count):
    return sorted(range(1, count), key=lambda bits: (bits == 1, bits))


def ffn_kernel(
    n_seq,
    n_mp,
    enc_ref,
    gain_ref,
    final_gain_ref,
    sel_ref,
    mask_ref,
    dec_ref,
    dec_gain_ref,
    fin_ref,
    fout_ref,
    wq_ref,
    wk_ref,
    wv_ref,
    wo_ref,
    out_ref,
    enc_all,
    normed,
    win,
    wout,
    hidden,
    part_out,
    part_in,
    z_out,
    z_in,
    enc_zs,
    enc_zr,
    enc_ps,
    enc_pr,
    in_s,
    in_r,
    out_s,
    out_r,
    red_ps,
    red_pr,
    red_zs,
    red_zr,
    local_sem,
    wq,
    wk,
    wv,
    wo,
    w_sem,
    dec_all,
    dec_normed,
    queries,
    enc_half,
    slot_out,
    slots,
    memory,
    keys,
    values,
    attended,
    att_out,
    att_in,
    dec_ps,
    dec_pr,
    slot_zs,
    slot_zr,
    slot_ps,
    slot_pr,
    att_ps,
    att_pr,
):
    s = lax.axis_index("seq")
    m = lax.axis_index("mp")
    rows, width = enc_ref.shape
    depth = fin_ref.shape[0]
    units = fin_ref.shape[1] // n_seq
    out_width = fout_ref.shape[1]
    total_rows = rows * n_seq
    per_block = out_width // width

    barrier = pltpu.get_barrier_semaphore()
    for bits in range(1, n_seq):
        pl.semaphore_signal(barrier, inc=1, device_id=(flip(s, bits), m), device_id_type=MESH)
    for bits in range(1, n_mp):
        pl.semaphore_signal(barrier, inc=1, device_id=(s, flip(m, bits)), device_id_type=MESH)
    pl.semaphore_wait(barrier, n_seq + n_mp - 2)

    my_rows = pl.ds(pl.multiple_of(s * rows, rows), rows)

    def plane_gather(buf, send_sem, recv_sem):
        def copy(slot, bits, peer):
            return pltpu.make_async_remote_copy(
                src_ref=buf.at[slot],
                dst_ref=buf.at[slot],
                send_sem=send_sem.at[bits],
                recv_sem=recv_sem.at[bits],
                device_id=(s, peer),
                device_id_type=MESH,
            )

        across = [bits for bits in range(n_mp - 2, 1, -2)]
        direct = {bits: copy(m, bits, flip(m, bits)) for bits in across + [1]}
        for bits in across + [1]:
            direct[bits].start()

        def finish():
            onward = []
            for bits in reversed(across):
                direct[bits].wait_recv()
                forward = copy(flip(m, bits), bits + 1, flip(m, 1))
                forward.start()
                onward.append(forward)
            direct[1].wait_recv()
            for forward in onward:
                forward.wait()
            for bits in across + [1]:
                direct[bits].wait_send()

        return finish

    def normalise(buf, dst, count, gain, gain_row):
        step = min(256, count)

        def body(i, carry):
            span = pl.ds(pl.multiple_of(i * step, step), step)
            squares = jnp.zeros((step, 1), jnp.float32)
            for k in range(n_mp):
                value = buf[k, span, :].astype(jnp.float32)
                squares = squares + jnp.sum(value * value, axis=1, keepdims=True)
            scale = lax.rsqrt(squares / (n_mp * width) + epsilon)
            for k in range(n_mp):
                cols = pl.ds(k * width, width)
                value = buf[k, span, :].astype(jnp.float32)
                dst[span, cols] = (value * scale * gain[pl.ds(gain_row, 1), cols]).astype(
                    jnp.bfloat16
                )
            return carry

        lax.fori_loop(0, count // step, body, 0)

    def product(left, right, layer, store):
        columns = right.shape[2]
        step = min(256, columns)

        def body(i, carry):
            cols = pl.ds(pl.multiple_of(i * step, step), step)
            store(
                cols, jnp.dot(left[...], right[layer, :, cols], preferred_element_type=jnp.float32)
            )
            return carry

        lax.fori_loop(0, columns // step, body, 0)

    def project_queries(layer):
        def store(cols, value):
            queries[:, cols] = (value * DH ** (-0.5)).astype(jnp.bfloat16)

        product(dec_normed, wq, layer, store)

    def project_memory(layer):
        def store_key(cols, value):
            keys[:, cols] = value.astype(jnp.bfloat16)

        def store_value(cols, value):
            values[:, cols] = value.astype(jnp.bfloat16)

        product(memory, wk, layer, store_key)
        product(memory, wv, layer, store_value)

    slot_rows = sel_ref.shape[0] // n_seq
    targets = dec_ref.shape[0]
    per_sentence = targets // n_seq
    layers = wq_ref.shape[0]
    heads = wq_ref.shape[2] // DH

    def attend():
        def body(i, carry):
            span = pl.ds(pl.multiple_of(i * per_sentence, per_sentence), per_sentence)
            slot_span = pl.ds(pl.multiple_of(i * slot_rows, slot_rows), slot_rows)
            live = mask_ref[i] > 0.5
            for head in range(heads):
                cols = pl.ds(head * DH, DH)
                scores = lax.dot_general(
                    queries[span, cols],
                    keys[slot_span, cols],
                    (((1,), (1,)), ((), ())),
                    preferred_element_type=jnp.float32,
                )
                scores = jnp.where(live, scores, -jnp.inf)
                top = jnp.max(scores, axis=1, keepdims=True)
                powers = jnp.exp(scores - top)
                weights = powers / jnp.sum(powers, axis=1, keepdims=True)
                attended[span, cols] = jnp.dot(
                    weights.astype(jnp.bfloat16),
                    values[slot_span, cols],
                    preferred_element_type=jnp.float32,
                ).astype(jnp.bfloat16)
            return carry

        lax.fori_loop(0, n_seq, body, 0)

    def att_copy(layer, slot, source):
        return pltpu.make_async_remote_copy(
            src_ref=att_out.at[layer, slot],
            dst_ref=att_in.at[layer, source],
            send_sem=att_ps.at[layer, slot],
            recv_sem=att_pr.at[layer, source],
            device_id=(s, slot),
            device_id_type=MESH,
        )

    def scatter_output(layer):
        step = max(width, 256)

        def body(i, carry):
            cols = pl.ds(pl.multiple_of(i * step, step), step)
            value = jnp.dot(
                attended[...], wo[layer, :, cols], preferred_element_type=jnp.float32
            ).astype(jnp.bfloat16)
            for j in range(step // width):
                att_out[layer, i * (step // width) + j] = value[:, j * width : (j + 1) * width]
            return carry

        lax.fori_loop(0, n_mp * width // step, body, 0)
        for bits in range(n_mp - 1, 0, -1):
            att_copy(layer, flip(m, bits), m).start()

    def collect_output(layer):
        total = att_out[layer, m].astype(jnp.float32)
        for bits in range(1, n_mp):
            peer = flip(m, bits)
            att_copy(layer, peer, peer).wait_recv()
            total = total + att_in[layer, peer].astype(jnp.float32)
        for bits in range(1, n_mp):
            att_copy(layer, flip(m, bits), m).wait_send()
        return total

    own_enc = pltpu.make_async_copy(enc_ref, enc_all.at[m, my_rows], local_sem.at[0])
    own_enc.start()
    enc_z = []
    for bits in z_order(n_seq):
        copy = pltpu.make_async_remote_copy(
            src_ref=enc_ref,
            dst_ref=enc_all.at[m, my_rows],
            send_sem=enc_zs.at[bits],
            recv_sem=enc_zr.at[bits],
            device_id=(flip(s, bits), m),
            device_id_type=MESH,
        )
        copy.start()
        enc_z.append(copy)

    own_in = pltpu.make_async_copy(
        fin_ref.at[:, pl.ds(pl.multiple_of(s * units, units), units)], win.at[s], local_sem.at[1]
    )
    own_in.start()
    own_out = pltpu.make_async_copy(
        fout_ref.at[pl.ds(pl.multiple_of(s * units, units), units)], wout.at[s], local_sem.at[2]
    )
    own_out.start()
    in_copies = []
    out_copies = []
    for bits in z_order(n_seq):
        peer = flip(s, bits)
        copy = pltpu.make_async_remote_copy(
            src_ref=fin_ref.at[:, pl.ds(pl.multiple_of(peer * units, units), units)],
            dst_ref=win.at[s],
            send_sem=in_s.at[bits],
            recv_sem=in_r.at[bits],
            device_id=(peer, m),
            device_id_type=MESH,
        )
        copy.start()
        in_copies.append(copy)
    for bits in z_order(n_seq):
        peer = flip(s, bits)
        copy = pltpu.make_async_remote_copy(
            src_ref=fout_ref.at[pl.ds(pl.multiple_of(peer * units, units), units)],
            dst_ref=wout.at[s],
            send_sem=out_s.at[bits],
            recv_sem=out_r.at[bits],
            device_id=(peer, m),
            device_id_type=MESH,
        )
        copy.start()
        out_copies.append(copy)

    weight_copies = []
    for index, (src, dst) in enumerate(((wq_ref, wq), (wk_ref, wk), (wv_ref, wv), (wo_ref, wo))):
        copy = pltpu.make_async_copy(src, dst, w_sem.at[index])
        copy.start()
        weight_copies.append(copy)
    own_dec = pltpu.make_async_copy(dec_ref, dec_all.at[0, m], local_sem.at[3])
    own_dec.start()
    own_dec.wait()
    finish_dec = plane_gather(dec_all.at[0], dec_ps.at[0], dec_pr.at[0])

    own_enc.wait()
    for copy in enc_z:
        copy.wait()

    enc_p = []
    for bits in range(1, n_mp):
        copy = pltpu.make_async_remote_copy(
            src_ref=enc_all.at[m],
            dst_ref=enc_all.at[m],
            send_sem=enc_ps.at[bits],
            recv_sem=enc_pr.at[bits],
            device_id=(s, flip(m, bits)),
            device_id_type=MESH,
        )
        copy.start()
        enc_p.append(copy)
    for copy in enc_p:
        copy.wait()

    chunk = min(256, rows)

    normalise(enc_all, normed, total_rows, gain_ref, 0)

    finish_dec()
    normalise(dec_all.at[0], dec_normed, targets, dec_gain_ref, 0)
    for copy in weight_copies:
        copy.wait()
    project_queries(0)

    own_in.wait()
    for copy in in_copies:
        copy.wait()

    tile = min(256, units)

    def hidden_chunk(i, carry):
        cols = pl.ds(pl.multiple_of((i % (units // tile)) * tile, tile), tile)
        span = pl.ds(pl.multiple_of((i // (units // tile)) * chunk, chunk), chunk)
        acc = jnp.zeros((chunk, tile), jnp.float32)
        for k in range(n_seq):
            acc = acc + jnp.dot(
                normed[span, pl.ds(k * depth, depth)],
                win[k, :, cols],
                preferred_element_type=jnp.float32,
            )
        hidden[span, cols] = jnp.maximum(acc, 0.0).astype(jnp.bfloat16)
        return carry

    lax.fori_loop(0, (total_rows // chunk) * (units // tile), hidden_chunk, 0)

    own_out.wait()

    def out_block(block):
        def rows_chunk(i, carry):
            span = pl.ds(pl.multiple_of(i * chunk, chunk), chunk)
            value = jnp.dot(hidden[span, :], wout[block], preferred_element_type=jnp.float32)
            for j in range(per_block):
                part_out[block * per_block + j, span, :] = value[
                    :, j * width : (j + 1) * width
                ].astype(jnp.bfloat16)
            return carry

        lax.fori_loop(0, total_rows // chunk, rows_chunk, 0)

    def send_copy(slot):
        return pltpu.make_async_remote_copy(
            src_ref=part_out.at[slot],
            dst_ref=part_in.at[m],
            send_sem=red_ps.at[slot],
            recv_sem=red_pr.at[m],
            device_id=(s, slot),
            device_id_type=MESH,
        )

    def send_block(block):
        out_block(block)
        for j in range(per_block):
            slot = block * per_block + j

            @pl.when(slot != m)
            def _():
                send_copy(slot).start()

    send_block(s)
    for bits, copy in zip(z_order(n_seq), out_copies):
        copy.wait()
        send_block(flip(s, bits))

    for bits in range(1, n_mp):
        send_copy(flip(m, bits)).wait_send()
    for bits in range(1, n_mp):
        peer = flip(m, bits)
        pltpu.make_async_remote_copy(
            src_ref=part_out.at[peer],
            dst_ref=part_in.at[peer],
            send_sem=red_ps.at[peer],
            recv_sem=red_pr.at[peer],
            device_id=(s, peer),
            device_id_type=MESH,
        ).wait_recv()

    def reduce_rows(block):
        span = pl.ds(pl.multiple_of(block * rows, rows), rows)
        total = part_out[m, span, :].astype(jnp.float32)
        for bits in range(1, n_mp):
            total = total + part_in[flip(m, bits), span, :].astype(jnp.float32)
        return total

    red_z = []
    for bits in z_order(n_seq):
        peer = flip(s, bits)
        z_out[bits] = reduce_rows(peer).astype(jnp.bfloat16)
        copy = pltpu.make_async_remote_copy(
            src_ref=z_out.at[bits],
            dst_ref=z_in.at[bits],
            send_sem=red_zs.at[bits],
            recv_sem=red_zr.at[bits],
            device_id=(peer, m),
            device_id_type=MESH,
        )
        copy.start()
        red_z.append(copy)
    total = reduce_rows(s)
    for bits, copy in zip(z_order(n_seq), red_z):
        copy.wait()
        total = total + z_in[bits].astype(jnp.float32)
    enc_half[...] = (enc_ref[...].astype(jnp.float32) + total).astype(jnp.bfloat16)

    def select(group):
        span = pl.ds(pl.multiple_of(group * slot_rows, slot_rows), slot_rows)
        return jnp.dot(
            sel_ref[span, :], enc_half[...], preferred_element_type=jnp.float32
        ).astype(jnp.bfloat16)

    my_slots = pl.ds(pl.multiple_of(s * slot_rows, slot_rows), slot_rows)
    slot_z = []
    for bits in z_order(n_seq):
        peer = flip(s, bits)
        slot_out[bits] = select(peer)
        copy = pltpu.make_async_remote_copy(
            src_ref=slot_out.at[bits],
            dst_ref=slots.at[m, my_slots],
            send_sem=slot_zs.at[bits],
            recv_sem=slot_zr.at[bits],
            device_id=(peer, m),
            device_id_type=MESH,
        )
        copy.start()
        slot_z.append(copy)
    slots[m, my_slots, :] = select(s)
    for copy in slot_z:
        copy.wait()

    plane_gather(slots, slot_ps, slot_pr)()
    normalise(slots, memory, n_seq * slot_rows, final_gain_ref, 0)
    project_memory(0)

    state = dec_ref[...].astype(jnp.float32)
    for layer in range(layers):
        if layer > 0:
            dec_all[layer, m] = state.astype(jnp.bfloat16)
            plane_gather(dec_all.at[layer], dec_ps.at[layer], dec_pr.at[layer])()
            normalise(dec_all.at[layer], dec_normed, targets, dec_gain_ref, layer)
            project_queries(layer)
        attend()
        scatter_output(layer)
        if layer + 1 < layers:
            project_memory(layer + 1)
        state = state + collect_output(layer)
    out_ref[...] = state.astype(out_ref.dtype)


def whole_fast(
    enc_rows,
    ffn_in,
    ffn_out,
    enc_gain,
    final_gain,
    select_rows,
    live,
    dec_rows,
    dec_gain,
    w_query,
    w_key,
    w_value,
    w_output,
):
    n_seq, n_mp = lax.axis_size("seq"), lax.axis_size("mp")
    rows, width = enc_rows.shape
    depth, units = ffn_in.shape[0], ffn_in.shape[1] // n_seq
    out_width = ffn_out.shape[1]
    total = rows * n_seq
    full = width * n_mp
    targets = dec_rows.shape[0]
    layers, _, heads_width = w_query.shape
    slot_total = select_rows.shape[0]
    half = jnp.bfloat16
    dma = pltpu.SemaphoreType.DMA
    return pl.pallas_call(
        functools.partial(ffn_kernel, n_seq, n_mp),
        out_shape=jax.ShapeDtypeStruct(dec_rows.shape, dec_rows.dtype),
        in_specs=[pl.BlockSpec(memory_space=pltpu.VMEM)] * 7
        + [pl.BlockSpec(memory_space=pl.ANY)] * 6,
        out_specs=pl.BlockSpec(memory_space=pltpu.VMEM),
        scratch_shapes=[
            pltpu.VMEM((n_mp, total, width), jnp.bfloat16),
            pltpu.VMEM((total, full), jnp.bfloat16),
            pltpu.VMEM((n_seq, depth, units), jnp.bfloat16),
            pltpu.VMEM((n_seq, units, out_width), jnp.bfloat16),
            pltpu.VMEM((total, units), jnp.bfloat16),
            pltpu.VMEM((n_mp, total, width), jnp.bfloat16),
            pltpu.VMEM((n_mp, total, width), jnp.bfloat16),
            pltpu.VMEM((n_seq, rows, width), jnp.bfloat16),
            pltpu.VMEM((n_seq, rows, width), jnp.bfloat16),
            dma((n_seq,)),
            dma((n_seq,)),
            dma((n_mp,)),
            dma((n_mp,)),
            dma((n_seq,)),
            dma((n_seq,)),
            dma((n_seq,)),
            dma((n_seq,)),
            dma((n_mp,)),
            dma((n_mp,)),
            dma((n_seq,)),
            dma((n_seq,)),
            dma((4,)),
            pltpu.VMEM(w_query.shape, half),
            pltpu.VMEM(w_key.shape, half),
            pltpu.VMEM(w_value.shape, half),
            pltpu.VMEM(w_output.shape, half),
            dma((4,)),
            pltpu.VMEM((layers, n_mp, targets, width), half),
            pltpu.VMEM((targets, full), half),
            pltpu.VMEM((targets, heads_width), half),
            pltpu.VMEM((rows, width), half),
            pltpu.VMEM((n_seq, slot_total // n_seq, width), half),
            pltpu.VMEM((n_mp, slot_total, width), half),
            pltpu.VMEM((slot_total, full), half),
            pltpu.VMEM((slot_total, heads_width), half),
            pltpu.VMEM((slot_total, heads_width), half),
            pltpu.VMEM((targets, heads_width), half),
            pltpu.VMEM((layers, n_mp, targets, width), half),
            pltpu.VMEM((layers, n_mp, targets, width), half),
            dma((layers, n_mp)),
            dma((layers, n_mp)),
            dma((n_seq,)),
            dma((n_seq,)),
            dma((n_mp,)),
            dma((n_mp,)),
            dma((layers, n_mp)),
            dma((layers, n_mp)),
        ],
        compiler_params=pltpu.CompilerParams(
            collective_id=0, has_side_effects=True, vmem_limit_bytes=60 * 1024 * 1024
        ),
    )(
        enc_rows,
        enc_gain.reshape(1, full),
        final_gain.reshape(1, full),
        select_rows,
        live,
        dec_rows,
        dec_gain,
        ffn_in,
        ffn_out,
        w_query,
        w_key,
        w_value,
        w_output,
    )


def fast_shapes(enc_rows, ffn_in, ffn_out, dec_rows, w_query):
    n_seq, n_mp = lax.axis_size("seq"), lax.axis_size("mp")
    power = (n_seq & (n_seq - 1)) == 0 and (n_mp & (n_mp - 1)) == 0
    aligned = (
        enc_rows.shape[1] % 128 == 0
        and ffn_in.shape[0] % 128 == 0
        and (ffn_in.shape[1] // n_seq) % 256 == 0
        and ffn_out.shape[1] % enc_rows.shape[1] == 0
        and enc_rows.shape[0] % 256 == 0
        and dec_rows.shape[0] % 256 == 0
        and (2 * enc_rows.shape[0] // n_seq) % 128 == 0
        and w_query.shape[2] % 256 == 0
        and w_query.shape[1] % 256 == 0
    )
    return power and aligned


def shards(
    enc_rows,
    ffn_in,
    ffn_out,
    enc_gain,
    final_gain,
    sent_lengths,
    group_table,
    dec_rows,
    dec_gain,
    w_query,
    w_key,
    w_value,
    w_output,
):
    group_count = lax.axis_size("seq")
    my_group = lax.axis_index("seq")
    col_width = enc_rows.shape[1]
    col_start = lax.axis_index("mp") * col_width
    row_count = enc_rows.shape[0]
    max_length = 2 * row_count // group_count
    fast = fast_shapes(enc_rows, ffn_in, ffn_out, dec_rows, w_query)
    if not fast:
        whole_rows = lax.all_gather(enc_rows, "mp", axis=1, tiled=True)
        normed = rms_scale(whole_rows.astype(jnp.float32), enc_gain).astype(jnp.bfloat16)
        full_in = lax.all_gather(ffn_in, "seq", axis=0, tiled=True)
        inner = jnp.dot(normed, full_in, preferred_element_type=jnp.float32)
        hidden = jnp.maximum(inner, 0.0).astype(jnp.bfloat16)
        partial_out = jnp.dot(
            hidden,
            lax.all_gather(ffn_out, "seq", axis=1, tiled=True),
            preferred_element_type=jnp.float32,
        )
    my_lengths = lax.dynamic_index_in_dim(sent_lengths, my_group, 0, keepdims=False)
    my_targets = lax.dynamic_index_in_dim(group_table, my_group, 0, keepdims=False)
    my_starts = jnp.cumsum(my_lengths) - my_lengths
    group_ids = jnp.arange(group_count, dtype=jnp.int32)
    matches = my_targets[None, :] == group_ids[:, None]
    send_starts = jnp.sum(jnp.where(matches, my_starts[None, :], 0), axis=1)
    positions = jnp.arange(max_length, dtype=jnp.int32)
    row_index = jnp.minimum(send_starts[:, None] + positions[None, :], row_count - 1)
    recv_lengths = jnp.sum(jnp.where(group_table == my_group, sent_lengths, 0), axis=1)
    live_mask = positions[None, :] < recv_lengths[:, None]
    if fast:
        select_rows = row_index.reshape(-1, 1) == jnp.arange(row_count, dtype=jnp.int32)[None, :]
        return whole_fast(
            enc_rows,
            ffn_in,
            ffn_out,
            enc_gain,
            final_gain,
            select_rows.astype(jnp.bfloat16),
            live_mask[:, None, :].astype(jnp.float32),
            dec_rows,
            dec_gain,
            w_query,
            w_key,
            w_value,
            w_output,
        )
    kv_width = w_key.shape[2]
    weight_list = []
    for layer_index in range(LAYERS):
        weight_list.append(w_key[layer_index])
        weight_list.append(w_value[layer_index])
    enc_share = lax.psum_scatter(partial_out, "mp", scatter_dimension=1, tiled=True)
    encoded = enc_rows.astype(jnp.float32) + enc_share
    squares = lax.psum(jnp.sum(encoded * encoded, axis=1), "mp")
    gain_part = lax.dynamic_slice_in_dim(final_gain, col_start, col_width, 0)
    memory = (encoded * lax.rsqrt(squares / D + epsilon)[:, None] * gain_part).astype(jnp.bfloat16)
    blocks = memory[row_index]
    gathered = lax.all_gather(
        lax.all_to_all(blocks, "seq", split_axis=0, concat_axis=0, tiled=True),
        "mp",
        axis=2,
        tiled=True,
    )
    projected = tuple(
        (
            jnp.einsum(
                "std,de->ste", gathered, weight_matrix, preferred_element_type=jnp.float32
            ).astype(jnp.bfloat16)
            for weight_matrix in weight_list
        )
    )
    tgt_rows = dec_rows.shape[0]
    per_sentence = tgt_rows // group_count
    local_heads = kv_width // DH
    final_state = dec_rows.astype(jnp.float32)
    for layer_index in range(LAYERS):
        state_half = lax.all_gather(final_state.astype(jnp.bfloat16), "mp", axis=1, tiled=True)
        normed_rows = rms_scale(state_half.astype(jnp.float32), dec_gain[layer_index]).astype(
            jnp.bfloat16
        )
        queries = (
            jnp.dot(normed_rows, w_query[layer_index], preferred_element_type=jnp.float32)
            * DH ** (-0.5)
        ).astype(jnp.bfloat16)
        query_heads = queries.reshape(group_count, per_sentence, local_heads, DH)
        key_heads = projected[2 * layer_index].reshape(group_count, max_length, local_heads, DH)
        value_heads = projected[2 * layer_index + 1].reshape(
            group_count, max_length, local_heads, DH
        )
        scores = jnp.einsum(
            "sqhd,sthd->shqt", query_heads, key_heads, preferred_element_type=jnp.float32
        )
        scores = jnp.where(live_mask[:, None, None, :], scores, -jnp.inf)
        weights = jax.nn.softmax(scores, axis=-1).astype(jnp.bfloat16)
        attended = jnp.einsum(
            "shqt,sthd->sqhd", weights, value_heads, preferred_element_type=jnp.float32
        ).astype(jnp.bfloat16)
        final_state = final_state + lax.psum_scatter(
            jnp.dot(
                attended.reshape(tgt_rows, kv_width),
                w_output[layer_index],
                preferred_element_type=jnp.float32,
            ).astype(jnp.bfloat16),
            "mp",
            scatter_dimension=1,
            tiled=True,
        ).astype(jnp.float32)
    return final_state.astype(jnp.bfloat16)


def solution(mesh):
    in_specs = (
        P("seq", "mp"),
        P("seq", "mp"),
        P("mp", "seq"),
        P(),
        P(),
        P(),
        P(),
        P("seq", "mp"),
        P(),
        P(None, None, "mp"),
        P(None, None, "mp"),
        P(None, None, "mp"),
        P(None, "mp", None),
    )
    out_specs = P("seq", "mp")
    return jax.shard_map(shards, mesh=mesh, in_specs=in_specs, out_specs=out_specs, check_vma=False)
```

```python
import functools

import jax
import jax.numpy as jnp
from jax import lax
from jax.experimental import pallas as pl
from jax.experimental.pallas import tpu as pltpu
from jax.sharding import PartitionSpec as P

MESH = pl.DeviceIdType.MESH

D = 1024
DH = 128
LAYERS = 2


epsilon = 1e-06


def rms_scale(values, gain_row):
    mean_square = jnp.mean(values * values, axis=-1, keepdims=True)
    return values * lax.rsqrt(mean_square + epsilon) * gain_row


def flip(index, bits):
    out = index
    for power in (1, 2, 4, 8, 16, 32):
        if bits & power:
            out = out + power - 2 * power * ((out // power) % 2)
    return out


def z_order(count):
    return sorted(range(1, count), key=lambda bits: (bits == 1, bits))


def ffn_kernel(
    n_seq,
    n_mp,
    enc_ref,
    gain_ref,
    final_gain_ref,
    lengths_ref,
    table_ref,
    dec_ref,
    dec_gain_ref,
    fin_ref,
    fout_ref,
    wq_ref,
    wk_ref,
    wv_ref,
    wo_ref,
    out_ref,
    enc_all,
    normed,
    win,
    wout,
    hidden,
    part_out,
    part_in,
    z_out,
    z_in,
    enc_zs,
    enc_zr,
    enc_ps,
    enc_pr,
    in_s,
    in_r,
    out_s,
    out_r,
    red_ps,
    red_pr,
    red_zs,
    red_zr,
    local_sem,
    wq,
    wk,
    wv,
    wo,
    w_sem,
    dec_all,
    dec_normed,
    queries,
    enc_half,
    slot_out,
    slots,
    memory,
    keys,
    values,
    attended,
    att_out,
    att_in,
    dec_ps,
    dec_pr,
    slot_zs,
    slot_zr,
    slot_ps,
    slot_pr,
    att_ps,
    att_pr,
    sel,
    mask,
    own_out_sem,
):
    s = lax.axis_index("seq")
    m = lax.axis_index("mp")
    rows, width = enc_ref.shape
    depth = fin_ref.shape[0]
    units = fin_ref.shape[1] // n_seq
    out_width = fout_ref.shape[1]
    total_rows = rows * n_seq
    per_block = out_width // width

    barrier = pltpu.get_barrier_semaphore()
    for bits in range(1, n_seq):
        pl.semaphore_signal(barrier, inc=1, device_id=(flip(s, bits), m), device_id_type=MESH)
    for bits in range(1, n_mp):
        pl.semaphore_signal(barrier, inc=1, device_id=(s, flip(m, bits)), device_id_type=MESH)
    pl.semaphore_wait(barrier, n_seq + n_mp - 2)

    my_rows = pl.ds(pl.multiple_of(s * rows, rows), rows)

    def plane_gather(buf, send_sem, recv_sem):
        def copy(slot, bits, peer):
            return pltpu.make_async_remote_copy(
                src_ref=buf.at[slot],
                dst_ref=buf.at[slot],
                send_sem=send_sem.at[bits],
                recv_sem=recv_sem.at[bits],
                device_id=(s, peer),
                device_id_type=MESH,
            )

        across = [bits for bits in range(n_mp - 2, 1, -2)]
        direct = {bits: copy(m, bits, flip(m, bits)) for bits in across + [1]}
        for bits in across + [1]:
            direct[bits].start()

        def finish():
            onward = []
            for bits in reversed(across):
                direct[bits].wait_recv()
                forward = copy(flip(m, bits), bits + 1, flip(m, 1))
                forward.start()
                onward.append(forward)
            direct[1].wait_recv()
            for forward in onward:
                forward.wait()
            for bits in across + [1]:
                direct[bits].wait_send()

        return finish

    def normalise(buf, dst, count, gain, gain_row):
        step = min(256, count)

        def body(i, carry):
            span = pl.ds(pl.multiple_of(i * step, step), step)
            squares = jnp.zeros((step, 1), jnp.float32)
            for k in range(n_mp):
                value = buf[k, span, :].astype(jnp.float32)
                squares = squares + jnp.sum(value * value, axis=1, keepdims=True)
            scale = lax.rsqrt(squares / (n_mp * width) + epsilon)
            for k in range(n_mp):
                cols = pl.ds(k * width, width)
                value = buf[k, span, :].astype(jnp.float32)
                dst[span, cols] = (value * scale * gain[pl.ds(gain_row, 1), cols]).astype(
                    jnp.bfloat16
                )
            return carry

        lax.fori_loop(0, count // step, body, 0)

    def product(left, right, layer, store):
        columns = right.shape[2]
        step = min(256, columns)

        def body(i, carry):
            cols = pl.ds(pl.multiple_of(i * step, step), step)
            store(
                cols, jnp.dot(left[...], right[layer, :, cols], preferred_element_type=jnp.float32)
            )
            return carry

        lax.fori_loop(0, columns // step, body, 0)

    def project_queries(layer):
        def store(cols, value):
            queries[:, cols] = (value * DH ** (-0.5)).astype(jnp.bfloat16)

        product(dec_normed, wq, layer, store)

    def project_memory(layer):
        def store_key(cols, value):
            keys[:, cols] = value.astype(jnp.bfloat16)

        def store_value(cols, value):
            values[:, cols] = value.astype(jnp.bfloat16)

        product(memory, wk, layer, store_key)
        product(memory, wv, layer, store_value)

    slot_rows = sel.shape[0] // n_seq
    targets = dec_ref.shape[0]
    per_sentence = targets // n_seq
    layers = wq_ref.shape[0]
    heads = wq_ref.shape[2] // DH

    def attend():
        def body(i, carry):
            span = pl.ds(pl.multiple_of(i * per_sentence, per_sentence), per_sentence)
            slot_span = pl.ds(pl.multiple_of(i * slot_rows, slot_rows), slot_rows)
            live = mask[i] > 0.5
            columns = [pl.ds(head * DH, DH) for head in range(heads)]
            scores = [
                lax.dot_general(
                    queries[span, cols],
                    keys[slot_span, cols],
                    (((1,), (1,)), ((), ())),
                    preferred_element_type=jnp.float32,
                )
                for cols in columns
            ]
            scores = [jnp.where(live, score, -jnp.inf) for score in scores]
            tops = [jnp.max(score, axis=1, keepdims=True) for score in scores]
            powers = [jnp.exp(score - top) for score, top in zip(scores, tops)]
            sums = [jnp.sum(power, axis=1, keepdims=True) for power in powers]
            weights = [(power / total).astype(jnp.bfloat16) for power, total in zip(powers, sums)]
            for cols, weight in zip(columns, weights):
                attended[span, cols] = jnp.dot(
                    weight, values[slot_span, cols], preferred_element_type=jnp.float32
                ).astype(jnp.bfloat16)
            return carry

        lax.fori_loop(0, n_seq, body, 0)

    def att_copy(layer, slot, source):
        return pltpu.make_async_remote_copy(
            src_ref=att_out.at[layer, slot],
            dst_ref=att_in.at[layer, source],
            send_sem=att_ps.at[layer, slot],
            recv_sem=att_pr.at[layer, source],
            device_id=(s, slot),
            device_id_type=MESH,
        )

    def scatter_output(layer):
        step = max(width, 256)

        def body(i, carry):
            cols = pl.ds(pl.multiple_of(i * step, step), step)
            value = jnp.dot(
                attended[...], wo[layer, :, cols], preferred_element_type=jnp.float32
            ).astype(jnp.bfloat16)
            for j in range(step // width):
                att_out[layer, i * (step // width) + j] = value[:, j * width : (j + 1) * width]
            return carry

        lax.fori_loop(0, n_mp * width // step, body, 0)
        for bits in range(n_mp - 1, 0, -1):
            att_copy(layer, flip(m, bits), m).start()

    def collect_output(layer):
        total = att_out[layer, m].astype(jnp.float32)
        for bits in range(1, n_mp):
            peer = flip(m, bits)
            att_copy(layer, peer, peer).wait_recv()
            total = total + att_in[layer, peer].astype(jnp.float32)
        for bits in range(1, n_mp):
            att_copy(layer, flip(m, bits), m).wait_send()
        return total

    own_enc = pltpu.make_async_copy(enc_ref, enc_all.at[m, my_rows], local_sem.at[0])
    own_enc.start()
    enc_z = []
    for bits in z_order(n_seq):
        copy = pltpu.make_async_remote_copy(
            src_ref=enc_ref,
            dst_ref=enc_all.at[m, my_rows],
            send_sem=enc_zs.at[bits],
            recv_sem=enc_zr.at[bits],
            device_id=(flip(s, bits), m),
            device_id_type=MESH,
        )
        copy.start()
        enc_z.append(copy)

    own_in = pltpu.make_async_copy(
        fin_ref.at[:, pl.ds(pl.multiple_of(s * units, units), units)], win.at[s], local_sem.at[1]
    )
    own_in.start()
    own_out = [
        pltpu.make_async_copy(
            fout_ref.at[
                pl.ds(pl.multiple_of(s * units, units), units), pl.ds(j * width, width)
            ],
            wout.at[s, j],
            own_out_sem.at[j],
        )
        for j in range(per_block)
    ]
    for copy in own_out:
        copy.start()
    in_copies = []
    for bits in z_order(n_seq):
        peer = flip(s, bits)
        copy = pltpu.make_async_remote_copy(
            src_ref=fin_ref.at[:, pl.ds(pl.multiple_of(peer * units, units), units)],
            dst_ref=win.at[s],
            send_sem=in_s.at[bits],
            recv_sem=in_r.at[bits],
            device_id=(peer, m),
            device_id_type=MESH,
        )
        copy.start()
        in_copies.append(copy)
    def out_copy(bits, peer, j):
        return pltpu.make_async_remote_copy(
            src_ref=fout_ref.at[
                pl.ds(pl.multiple_of(peer * units, units), units), pl.ds(j * width, width)
            ],
            dst_ref=wout.at[s, j],
            send_sem=out_s.at[bits, j],
            recv_sem=out_r.at[bits, j],
            device_id=(peer, m),
            device_id_type=MESH,
        )

    for j in range(per_block):
        out_copy(1, flip(s, 1), j).start()
    for j in range(per_block):
        for bits in range(2, n_seq):
            out_copy(bits, flip(s, bits), j).start()

    weight_copies = []
    for index, (src, dst) in enumerate(((wq_ref, wq), (wk_ref, wk), (wv_ref, wv), (wo_ref, wo))):
        copy = pltpu.make_async_copy(src, dst, w_sem.at[index])
        copy.start()
        weight_copies.append(copy)
    own_dec = pltpu.make_async_copy(dec_ref, dec_all.at[0, m], local_sem.at[3])
    own_dec.start()
    own_dec.wait()
    finish_dec = plane_gather(dec_all.at[0], dec_ps.at[0], dec_pr.at[0])

    own_enc.wait()
    for copy in enc_z:
        copy.wait()

    enc_p = []
    for bits in range(1, n_mp):
        copy = pltpu.make_async_remote_copy(
            src_ref=enc_all.at[m],
            dst_ref=enc_all.at[m],
            send_sem=enc_ps.at[bits],
            recv_sem=enc_pr.at[bits],
            device_id=(s, flip(m, bits)),
            device_id_type=MESH,
        )
        copy.start()
        enc_p.append(copy)
    for copy in enc_p:
        copy.wait()

    chunk = min(256, rows)

    normalise(enc_all, normed, total_rows, gain_ref, 0)

    for group in range(n_seq):
        start = jnp.int32(0)
        before = jnp.int32(0)
        for j in range(n_seq):
            start = start + jnp.where(table_ref[s, j] == group, before, 0)
            before = before + lengths_ref[s, j]
        position = lax.broadcasted_iota(jnp.int32, (slot_rows, rows), 0)
        column = lax.broadcasted_iota(jnp.int32, (slot_rows, rows), 1)
        wanted = jnp.minimum(position + start, rows - 1)
        sel[pl.ds(group * slot_rows, slot_rows), :] = jnp.where(wanted == column, 1.0, 0.0).astype(
            jnp.bfloat16
        )
    for source in range(n_seq):
        length = jnp.int32(0)
        for j in range(n_seq):
            length = length + jnp.where(table_ref[source, j] == s, lengths_ref[source, j], 0)
        slot = lax.broadcasted_iota(jnp.int32, (1, slot_rows), 1)
        mask[source] = jnp.where(slot < length, 1.0, 0.0)

    finish_dec()
    normalise(dec_all.at[0], dec_normed, targets, dec_gain_ref, 0)
    for copy in weight_copies:
        copy.wait()
    project_queries(0)

    own_in.wait()
    for copy in in_copies:
        copy.wait()

    tile = min(256, units)

    def hidden_chunk(i, carry):
        cols = pl.ds(pl.multiple_of((i % (units // tile)) * tile, tile), tile)
        span = pl.ds(pl.multiple_of((i // (units // tile)) * chunk, chunk), chunk)
        acc = jnp.zeros((chunk, tile), jnp.float32)
        for k in range(n_seq):
            acc = acc + jnp.dot(
                normed[span, pl.ds(k * depth, depth)],
                win[k, :, cols],
                preferred_element_type=jnp.float32,
            )
        hidden[span, cols] = jnp.maximum(acc, 0.0).astype(jnp.bfloat16)
        return carry

    lax.fori_loop(0, (total_rows // chunk) * (units // tile), hidden_chunk, 0)

    def send_copy(slot, span):
        return pltpu.make_async_remote_copy(
            src_ref=part_out.at[slot, span],
            dst_ref=part_in.at[m, span],
            send_sem=red_ps.at[slot],
            recv_sem=red_pr.at[m],
            device_id=(s, slot),
            device_id_type=MESH,
        )

    def send_block(block, j):
        slot = block * per_block + j

        def rows_chunk(i, carry):
            span = pl.ds(pl.multiple_of(i * chunk, chunk), chunk)
            part_out[slot, span, :] = jnp.dot(
                hidden[span, :], wout[block, j], preferred_element_type=jnp.float32
            ).astype(jnp.bfloat16)

            @pl.when(slot != m)
            def _():
                send_copy(slot, span).start()

            return carry

        lax.fori_loop(0, total_rows // chunk, rows_chunk, 0)

    def receive_block(bits, j):
        peer = flip_any(bits)
        out_copy(bits, peer, j).wait()
        send_block(peer, j)

    inner = (s % 2 + s // 2) % 2

    def flip_any(bits):
        if isinstance(bits, int):
            return flip(s, bits)
        return flip(s, 2) * (3 - bits) + flip(s, 3) * (bits - 2)

    later = list(range(2, n_seq))
    if n_seq == 4:
        later = [2 + inner, 3 - inner]
    for j in range(per_block):
        own_out[j].wait()
        send_block(s, j)
    for j in range(per_block):
        receive_block(1, j)
    for j in range(per_block):
        for bits in later:
            receive_block(bits, j)

    everything = pl.ds(0, total_rows)
    for bits in range(1, n_mp):
        send_copy(flip(m, bits), everything).wait_send()
    for bits in range(1, n_mp):
        peer = flip(m, bits)
        pltpu.make_async_remote_copy(
            src_ref=part_out.at[peer],
            dst_ref=part_in.at[peer],
            send_sem=red_ps.at[peer],
            recv_sem=red_pr.at[peer],
            device_id=(s, peer),
            device_id_type=MESH,
        ).wait_recv()

    def reduce_rows(block):
        span = pl.ds(pl.multiple_of(block * rows, rows), rows)
        total = part_out[m, span, :].astype(jnp.float32)
        for bits in range(1, n_mp):
            total = total + part_in[flip(m, bits), span, :].astype(jnp.float32)
        return total

    red_z = []
    for bits in z_order(n_seq):
        peer = flip(s, bits)
        z_out[bits] = reduce_rows(peer).astype(jnp.bfloat16)
        copy = pltpu.make_async_remote_copy(
            src_ref=z_out.at[bits],
            dst_ref=z_in.at[bits],
            send_sem=red_zs.at[bits],
            recv_sem=red_zr.at[bits],
            device_id=(peer, m),
            device_id_type=MESH,
        )
        copy.start()
        red_z.append(copy)
    total = reduce_rows(s)
    for bits, copy in zip(z_order(n_seq), red_z):
        copy.wait()
        total = total + z_in[bits].astype(jnp.float32)
    enc_half[...] = (enc_ref[...].astype(jnp.float32) + total).astype(jnp.bfloat16)

    def select(group):
        span = pl.ds(pl.multiple_of(group * slot_rows, slot_rows), slot_rows)
        return jnp.dot(
            sel[span, :], enc_half[...], preferred_element_type=jnp.float32
        ).astype(jnp.bfloat16)

    my_slots = pl.ds(pl.multiple_of(s * slot_rows, slot_rows), slot_rows)
    slot_z = []
    for bits in z_order(n_seq):
        peer = flip(s, bits)
        slot_out[bits] = select(peer)
        copy = pltpu.make_async_remote_copy(
            src_ref=slot_out.at[bits],
            dst_ref=slots.at[m, my_slots],
            send_sem=slot_zs.at[bits],
            recv_sem=slot_zr.at[bits],
            device_id=(peer, m),
            device_id_type=MESH,
        )
        copy.start()
        slot_z.append(copy)
    slots[m, my_slots, :] = select(s)
    for copy in slot_z:
        copy.wait()

    plane_gather(slots, slot_ps, slot_pr)()
    normalise(slots, memory, n_seq * slot_rows, final_gain_ref, 0)
    project_memory(0)

    state = dec_ref[...].astype(jnp.float32)
    for layer in range(layers):
        if layer > 0:
            dec_all[layer, m] = state.astype(jnp.bfloat16)
            plane_gather(dec_all.at[layer], dec_ps.at[layer], dec_pr.at[layer])()
            normalise(dec_all.at[layer], dec_normed, targets, dec_gain_ref, layer)
            project_queries(layer)
        attend()
        scatter_output(layer)
        if layer + 1 < layers:
            project_memory(layer + 1)
        state = state + collect_output(layer)
    out_ref[...] = state.astype(out_ref.dtype)


def whole_fast(
    enc_rows,
    ffn_in,
    ffn_out,
    enc_gain,
    final_gain,
    sent_lengths,
    group_table,
    dec_rows,
    dec_gain,
    w_query,
    w_key,
    w_value,
    w_output,
):
    n_seq, n_mp = lax.axis_size("seq"), lax.axis_size("mp")
    rows, width = enc_rows.shape
    depth, units = ffn_in.shape[0], ffn_in.shape[1] // n_seq
    out_width = ffn_out.shape[1]
    total = rows * n_seq
    full = width * n_mp
    targets = dec_rows.shape[0]
    layers, _, heads_width = w_query.shape
    slot_total = 2 * rows
    per_block = out_width // width
    half = jnp.bfloat16
    dma = pltpu.SemaphoreType.DMA
    return pl.pallas_call(
        functools.partial(ffn_kernel, n_seq, n_mp),
        out_shape=jax.ShapeDtypeStruct(dec_rows.shape, dec_rows.dtype),
        in_specs=[pl.BlockSpec(memory_space=pltpu.VMEM)] * 3
        + [pl.BlockSpec(memory_space=pltpu.SMEM)] * 2
        + [pl.BlockSpec(memory_space=pltpu.VMEM)] * 2
        + [pl.BlockSpec(memory_space=pl.ANY)] * 6,
        out_specs=pl.BlockSpec(memory_space=pltpu.VMEM),
        scratch_shapes=[
            pltpu.VMEM((n_mp, total, width), jnp.bfloat16),
            pltpu.VMEM((total, full), jnp.bfloat16),
            pltpu.VMEM((n_seq, depth, units), jnp.bfloat16),
            pltpu.VMEM((n_seq, per_block, units, width), jnp.bfloat16),
            pltpu.VMEM((total, units), jnp.bfloat16),
            pltpu.VMEM((n_mp, total, width), jnp.bfloat16),
            pltpu.VMEM((n_mp, total, width), jnp.bfloat16),
            pltpu.VMEM((n_seq, rows, width), jnp.bfloat16),
            pltpu.VMEM((n_seq, rows, width), jnp.bfloat16),
            dma((n_seq,)),
            dma((n_seq,)),
            dma((n_mp,)),
            dma((n_mp,)),
            dma((n_seq,)),
            dma((n_seq,)),
            dma((n_seq, per_block)),
            dma((n_seq, per_block)),
            dma((n_mp,)),
            dma((n_mp,)),
            dma((n_seq,)),
            dma((n_seq,)),
            dma((4,)),
            pltpu.VMEM(w_query.shape, half),
            pltpu.VMEM(w_key.shape, half),
            pltpu.VMEM(w_value.shape, half),
            pltpu.VMEM(w_output.shape, half),
            dma((4,)),
            pltpu.VMEM((layers, n_mp, targets, width), half),
            pltpu.VMEM((targets, full), half),
            pltpu.VMEM((targets, heads_width), half),
            pltpu.VMEM((rows, width), half),
            pltpu.VMEM((n_seq, slot_total // n_seq, width), half),
            pltpu.VMEM((n_mp, slot_total, width), half),
            pltpu.VMEM((slot_total, full), half),
            pltpu.VMEM((slot_total, heads_width), half),
            pltpu.VMEM((slot_total, heads_width), half),
            pltpu.VMEM((targets, heads_width), half),
            pltpu.VMEM((layers, n_mp, targets, width), half),
            pltpu.VMEM((layers, n_mp, targets, width), half),
            dma((layers, n_mp)),
            dma((layers, n_mp)),
            dma((n_seq,)),
            dma((n_seq,)),
            dma((n_mp,)),
            dma((n_mp,)),
            dma((layers, n_mp)),
            dma((layers, n_mp)),
            pltpu.VMEM((slot_total, rows), half),
            pltpu.VMEM((n_seq, 1, slot_total // n_seq), jnp.float32),
            dma((per_block,)),
        ],
        compiler_params=pltpu.CompilerParams(
            collective_id=0, has_side_effects=True, vmem_limit_bytes=60 * 1024 * 1024
        ),
    )(
        enc_rows,
        enc_gain.reshape(1, full),
        final_gain.reshape(1, full),
        sent_lengths,
        group_table,
        dec_rows,
        dec_gain,
        ffn_in,
        ffn_out,
        w_query,
        w_key,
        w_value,
        w_output,
    )


def fast_shapes(enc_rows, ffn_in, ffn_out, dec_rows, w_query):
    n_seq, n_mp = lax.axis_size("seq"), lax.axis_size("mp")
    power = (n_seq & (n_seq - 1)) == 0 and (n_mp & (n_mp - 1)) == 0
    aligned = (
        enc_rows.shape[1] % 128 == 0
        and ffn_in.shape[0] % 128 == 0
        and (ffn_in.shape[1] // n_seq) % 256 == 0
        and ffn_out.shape[1] % enc_rows.shape[1] == 0
        and enc_rows.shape[0] % 256 == 0
        and dec_rows.shape[0] % 256 == 0
        and (2 * enc_rows.shape[0] // n_seq) % 128 == 0
        and w_query.shape[2] % 256 == 0
        and w_query.shape[1] % 256 == 0
    )
    return power and aligned


def shards(
    enc_rows,
    ffn_in,
    ffn_out,
    enc_gain,
    final_gain,
    sent_lengths,
    group_table,
    dec_rows,
    dec_gain,
    w_query,
    w_key,
    w_value,
    w_output,
):
    group_count = lax.axis_size("seq")
    my_group = lax.axis_index("seq")
    col_width = enc_rows.shape[1]
    col_start = lax.axis_index("mp") * col_width
    row_count = enc_rows.shape[0]
    max_length = 2 * row_count // group_count
    fast = fast_shapes(enc_rows, ffn_in, ffn_out, dec_rows, w_query)
    if not fast:
        whole_rows = lax.all_gather(enc_rows, "mp", axis=1, tiled=True)
        normed = rms_scale(whole_rows.astype(jnp.float32), enc_gain).astype(jnp.bfloat16)
        full_in = lax.all_gather(ffn_in, "seq", axis=0, tiled=True)
        inner = jnp.dot(normed, full_in, preferred_element_type=jnp.float32)
        hidden = jnp.maximum(inner, 0.0).astype(jnp.bfloat16)
        partial_out = jnp.dot(
            hidden,
            lax.all_gather(ffn_out, "seq", axis=1, tiled=True),
            preferred_element_type=jnp.float32,
        )
    my_lengths = lax.dynamic_index_in_dim(sent_lengths, my_group, 0, keepdims=False)
    my_targets = lax.dynamic_index_in_dim(group_table, my_group, 0, keepdims=False)
    my_starts = jnp.cumsum(my_lengths) - my_lengths
    group_ids = jnp.arange(group_count, dtype=jnp.int32)
    matches = my_targets[None, :] == group_ids[:, None]
    send_starts = jnp.sum(jnp.where(matches, my_starts[None, :], 0), axis=1)
    positions = jnp.arange(max_length, dtype=jnp.int32)
    row_index = jnp.minimum(send_starts[:, None] + positions[None, :], row_count - 1)
    recv_lengths = jnp.sum(jnp.where(group_table == my_group, sent_lengths, 0), axis=1)
    live_mask = positions[None, :] < recv_lengths[:, None]
    if fast:
        return whole_fast(
            enc_rows,
            ffn_in,
            ffn_out,
            enc_gain,
            final_gain,
            sent_lengths,
            group_table,
            dec_rows,
            dec_gain,
            w_query,
            w_key,
            w_value,
            w_output,
        )
    kv_width = w_key.shape[2]
    weight_list = []
    for layer_index in range(LAYERS):
        weight_list.append(w_key[layer_index])
        weight_list.append(w_value[layer_index])
    enc_share = lax.psum_scatter(partial_out, "mp", scatter_dimension=1, tiled=True)
    encoded = enc_rows.astype(jnp.float32) + enc_share
    squares = lax.psum(jnp.sum(encoded * encoded, axis=1), "mp")
    gain_part = lax.dynamic_slice_in_dim(final_gain, col_start, col_width, 0)
    memory = (encoded * lax.rsqrt(squares / D + epsilon)[:, None] * gain_part).astype(jnp.bfloat16)
    blocks = memory[row_index]
    gathered = lax.all_gather(
        lax.all_to_all(blocks, "seq", split_axis=0, concat_axis=0, tiled=True),
        "mp",
        axis=2,
        tiled=True,
    )
    projected = tuple(
        (
            jnp.einsum(
                "std,de->ste", gathered, weight_matrix, preferred_element_type=jnp.float32
            ).astype(jnp.bfloat16)
            for weight_matrix in weight_list
        )
    )
    tgt_rows = dec_rows.shape[0]
    per_sentence = tgt_rows // group_count
    local_heads = kv_width // DH
    final_state = dec_rows.astype(jnp.float32)
    for layer_index in range(LAYERS):
        state_half = lax.all_gather(final_state.astype(jnp.bfloat16), "mp", axis=1, tiled=True)
        normed_rows = rms_scale(state_half.astype(jnp.float32), dec_gain[layer_index]).astype(
            jnp.bfloat16
        )
        queries = (
            jnp.dot(normed_rows, w_query[layer_index], preferred_element_type=jnp.float32)
            * DH ** (-0.5)
        ).astype(jnp.bfloat16)
        query_heads = queries.reshape(group_count, per_sentence, local_heads, DH)
        key_heads = projected[2 * layer_index].reshape(group_count, max_length, local_heads, DH)
        value_heads = projected[2 * layer_index + 1].reshape(
            group_count, max_length, local_heads, DH
        )
        scores = jnp.einsum(
            "sqhd,sthd->shqt", query_heads, key_heads, preferred_element_type=jnp.float32
        )
        scores = jnp.where(live_mask[:, None, None, :], scores, -jnp.inf)
        weights = jax.nn.softmax(scores, axis=-1).astype(jnp.bfloat16)
        attended = jnp.einsum(
            "shqt,sthd->sqhd", weights, value_heads, preferred_element_type=jnp.float32
        ).astype(jnp.bfloat16)
        final_state = final_state + lax.psum_scatter(
            jnp.dot(
                attended.reshape(tgt_rows, kv_width),
                w_output[layer_index],
                preferred_element_type=jnp.float32,
            ).astype(jnp.bfloat16),
            "mp",
            scatter_dimension=1,
            tiled=True,
        ).astype(jnp.float32)
    return final_state.astype(jnp.bfloat16)


def solution(mesh):
    in_specs = (
        P("seq", "mp"),
        P("seq", "mp"),
        P("mp", "seq"),
        P(),
        P(),
        P(),
        P(),
        P("seq", "mp"),
        P(),
        P(None, None, "mp"),
        P(None, None, "mp"),
        P(None, None, "mp"),
        P(None, "mp", None),
    )
    out_specs = P("seq", "mp")
    return jax.shard_map(shards, mesh=mesh, in_specs=in_specs, out_specs=out_specs, check_vma=False)
```

```python
import functools

import jax
import jax.numpy as jnp
from jax import lax
from jax.experimental import pallas as pl
from jax.experimental.pallas import tpu as pltpu
from jax.sharding import PartitionSpec as P

MESH = pl.DeviceIdType.MESH

D = 1024
DH = 128
LAYERS = 2


epsilon = 1e-06


def rms_scale(values, gain_row):
    mean_square = jnp.mean(values * values, axis=-1, keepdims=True)
    return values * lax.rsqrt(mean_square + epsilon) * gain_row


def flip(index, bits):
    out = index
    for power in (1, 2, 4, 8, 16, 32):
        if bits & power:
            out = out + power - 2 * power * ((out // power) % 2)
    return out


def z_order(count):
    return sorted(range(1, count), key=lambda bits: (bits == 1, bits))


def ffn_kernel(
    n_seq,
    n_mp,
    enc_ref,
    gain_ref,
    final_gain_ref,
    lengths_ref,
    table_ref,
    dec_ref,
    dec_gain_ref,
    fin_ref,
    fout_ref,
    wq_ref,
    wk_ref,
    wv_ref,
    wo_ref,
    out_ref,
    enc_all,
    normed,
    win,
    wout,
    hidden,
    part_out,
    part_in,
    z_out,
    z_in,
    enc_zs,
    enc_zr,
    enc_ps,
    enc_pr,
    in_s,
    in_r,
    out_s,
    out_r,
    red_ps,
    red_pr,
    red_zs,
    red_zr,
    local_sem,
    wq,
    wk,
    wv,
    wo,
    w_sem,
    dec_all,
    dec_normed,
    queries,
    enc_half,
    slot_out,
    slots,
    memory,
    keys,
    values,
    attended,
    att_out,
    att_in,
    dec_ps,
    dec_pr,
    slot_zs,
    slot_zr,
    slot_ps,
    slot_pr,
    att_ps,
    att_pr,
    sel,
    mask,
    own_out_sem,
):
    s = lax.axis_index("seq")
    m = lax.axis_index("mp")
    rows, width = enc_ref.shape
    depth = fin_ref.shape[0]
    units = fin_ref.shape[1] // n_seq
    out_width = fout_ref.shape[1]
    total_rows = rows * n_seq
    per_block = out_width // width

    barrier = pltpu.get_barrier_semaphore()
    for bits in range(1, n_seq):
        pl.semaphore_signal(barrier, inc=1, device_id=(flip(s, bits), m), device_id_type=MESH)
    for bits in range(1, n_mp):
        pl.semaphore_signal(barrier, inc=1, device_id=(s, flip(m, bits)), device_id_type=MESH)
    pl.semaphore_wait(barrier, n_seq + n_mp - 2)

    my_rows = pl.ds(pl.multiple_of(s * rows, rows), rows)

    def plane_gather(buf, send_sem, recv_sem):
        def copy(slot, bits, peer):
            return pltpu.make_async_remote_copy(
                src_ref=buf.at[slot],
                dst_ref=buf.at[slot],
                send_sem=send_sem.at[bits],
                recv_sem=recv_sem.at[bits],
                device_id=(s, peer),
                device_id_type=MESH,
            )

        across = [bits for bits in range(n_mp - 2, 1, -2)]
        direct = {bits: copy(m, bits, flip(m, bits)) for bits in across + [1]}
        for bits in across + [1]:
            direct[bits].start()

        def finish():
            onward = []
            for bits in reversed(across):
                direct[bits].wait_recv()
                forward = copy(flip(m, bits), bits + 1, flip(m, 1))
                forward.start()
                onward.append(forward)
            direct[1].wait_recv()
            for forward in onward:
                forward.wait()
            for bits in across + [1]:
                direct[bits].wait_send()

        return finish

    def normalise(buf, dst, count, gain, gain_row):
        step = min(256, count)

        def body(i, carry):
            span = pl.ds(pl.multiple_of(i * step, step), step)
            squares = jnp.zeros((step, 1), jnp.float32)
            for k in range(n_mp):
                value = buf[k, span, :].astype(jnp.float32)
                squares = squares + jnp.sum(value * value, axis=1, keepdims=True)
            scale = lax.rsqrt(squares / (n_mp * width) + epsilon)
            for k in range(n_mp):
                cols = pl.ds(k * width, width)
                value = buf[k, span, :].astype(jnp.float32)
                dst[span, cols] = (value * scale * gain[pl.ds(gain_row, 1), cols]).astype(
                    jnp.bfloat16
                )
            return carry

        lax.fori_loop(0, count // step, body, 0)

    def product(left, right, layer, store):
        columns = right.shape[2]
        step = min(256, columns)

        def body(i, carry):
            cols = pl.ds(pl.multiple_of(i * step, step), step)
            store(
                cols, jnp.dot(left[...], right[layer, :, cols], preferred_element_type=jnp.float32)
            )
            return carry

        lax.fori_loop(0, columns // step, body, 0)

    def project_queries(layer):
        def store(cols, value):
            queries[:, cols] = (value * DH ** (-0.5)).astype(jnp.bfloat16)

        product(dec_normed, wq, layer, store)

    def project_memory(layer):
        def store_key(cols, value):
            keys[:, cols] = value.astype(jnp.bfloat16)

        def store_value(cols, value):
            values[:, cols] = value.astype(jnp.bfloat16)

        product(memory, wk, layer, store_key)
        product(memory, wv, layer, store_value)

    slot_rows = sel.shape[0] // n_seq
    targets = dec_ref.shape[0]
    per_sentence = targets // n_seq
    layers = wq_ref.shape[0]
    heads = wq_ref.shape[2] // DH

    def attend():
        def body(i, carry):
            span = pl.ds(pl.multiple_of(i * per_sentence, per_sentence), per_sentence)
            slot_span = pl.ds(pl.multiple_of(i * slot_rows, slot_rows), slot_rows)
            live = mask[i] > 0.5
            columns = [pl.ds(head * DH, DH) for head in range(heads)]
            scores = [
                lax.dot_general(
                    queries[span, cols],
                    keys[slot_span, cols],
                    (((1,), (1,)), ((), ())),
                    preferred_element_type=jnp.float32,
                )
                for cols in columns
            ]
            scores = [jnp.where(live, score, -jnp.inf) for score in scores]
            tops = [jnp.max(score, axis=1, keepdims=True) for score in scores]
            powers = [jnp.exp(score - top) for score, top in zip(scores, tops)]
            sums = [jnp.sum(power, axis=1, keepdims=True) for power in powers]
            weights = [(power / total).astype(jnp.bfloat16) for power, total in zip(powers, sums)]
            for cols, weight in zip(columns, weights):
                attended[span, cols] = jnp.dot(
                    weight, values[slot_span, cols], preferred_element_type=jnp.float32
                ).astype(jnp.bfloat16)
            return carry

        lax.fori_loop(0, n_seq, body, 0, unroll=n_seq <= 4)

    def att_copy(layer, slot, source):
        return pltpu.make_async_remote_copy(
            src_ref=att_out.at[layer, slot],
            dst_ref=att_in.at[layer, source],
            send_sem=att_ps.at[layer, slot],
            recv_sem=att_pr.at[layer, source],
            device_id=(s, slot),
            device_id_type=MESH,
        )

    def scatter_output(layer):
        step = max(width, 256)

        def body(i, carry):
            chip = (i + m // (step // width) + 1) % (n_mp * width // step)
            cols = pl.ds(pl.multiple_of(chip * step, step), step)
            value = jnp.dot(
                attended[...], wo[layer, :, cols], preferred_element_type=jnp.float32
            ).astype(jnp.bfloat16)
            for j in range(step // width):
                slot = chip * (step // width) + j
                att_out[layer, slot] = value[:, j * width : (j + 1) * width]

                @pl.when(slot != m)
                def _():
                    att_copy(layer, slot, m).start()

            return carry

        lax.fori_loop(0, n_mp * width // step, body, 0)

    def collect_output(layer):
        total = att_out[layer, m].astype(jnp.float32)
        for bits in range(1, n_mp):
            peer = flip(m, bits)
            att_copy(layer, peer, peer).wait_recv()
            total = total + att_in[layer, peer].astype(jnp.float32)
        for bits in range(1, n_mp):
            att_copy(layer, flip(m, bits), m).wait_send()
        return total

    own_enc = pltpu.make_async_copy(enc_ref, enc_all.at[m, my_rows], local_sem.at[0])
    own_enc.start()
    enc_z = []
    for bits in z_order(n_seq):
        copy = pltpu.make_async_remote_copy(
            src_ref=enc_ref,
            dst_ref=enc_all.at[m, my_rows],
            send_sem=enc_zs.at[bits],
            recv_sem=enc_zr.at[bits],
            device_id=(flip(s, bits), m),
            device_id_type=MESH,
        )
        copy.start()
        enc_z.append(copy)

    own_in = pltpu.make_async_copy(
        fin_ref.at[:, pl.ds(pl.multiple_of(s * units, units), units)], win.at[s], local_sem.at[1]
    )
    own_in.start()
    own_out = [
        pltpu.make_async_copy(
            fout_ref.at[
                pl.ds(pl.multiple_of(s * units, units), units), pl.ds(j * width, width)
            ],
            wout.at[s, j],
            own_out_sem.at[j],
        )
        for j in range(per_block)
    ]
    for copy in own_out:
        copy.start()
    in_copies = []
    for bits in z_order(n_seq):
        peer = flip(s, bits)
        copy = pltpu.make_async_remote_copy(
            src_ref=fin_ref.at[:, pl.ds(pl.multiple_of(peer * units, units), units)],
            dst_ref=win.at[s],
            send_sem=in_s.at[bits],
            recv_sem=in_r.at[bits],
            device_id=(peer, m),
            device_id_type=MESH,
        )
        copy.start()
        in_copies.append(copy)
    def out_copy(bits, peer, j):
        return pltpu.make_async_remote_copy(
            src_ref=fout_ref.at[
                pl.ds(pl.multiple_of(peer * units, units), units), pl.ds(j * width, width)
            ],
            dst_ref=wout.at[s, j],
            send_sem=out_s.at[bits, j],
            recv_sem=out_r.at[bits, j],
            device_id=(peer, m),
            device_id_type=MESH,
        )

    for j in range(per_block):
        out_copy(1, flip(s, 1), j).start()
    for j in range(per_block):
        for bits in range(2, n_seq):
            out_copy(bits, flip(s, bits), j).start()

    weight_copies = []
    for index, (src, dst) in enumerate(((wq_ref, wq), (wk_ref, wk), (wv_ref, wv), (wo_ref, wo))):
        copy = pltpu.make_async_copy(src, dst, w_sem.at[index])
        copy.start()
        weight_copies.append(copy)
    own_dec = pltpu.make_async_copy(dec_ref, dec_all.at[0, m], local_sem.at[3])
    own_dec.start()
    own_dec.wait()
    finish_dec = plane_gather(dec_all.at[0], dec_ps.at[0], dec_pr.at[0])

    own_enc.wait()
    for copy in enc_z:
        copy.wait()

    enc_p = []
    for bits in range(1, n_mp):
        copy = pltpu.make_async_remote_copy(
            src_ref=enc_all.at[m],
            dst_ref=enc_all.at[m],
            send_sem=enc_ps.at[bits],
            recv_sem=enc_pr.at[bits],
            device_id=(s, flip(m, bits)),
            device_id_type=MESH,
        )
        copy.start()
        enc_p.append(copy)
    for copy in enc_p:
        copy.wait()

    chunk = min(256, rows)

    normalise(enc_all, normed, total_rows, gain_ref, 0)

    for group in range(n_seq):
        start = jnp.int32(0)
        before = jnp.int32(0)
        for j in range(n_seq):
            start = start + jnp.where(table_ref[s, j] == group, before, 0)
            before = before + lengths_ref[s, j]
        position = lax.broadcasted_iota(jnp.int32, (slot_rows, rows), 0)
        column = lax.broadcasted_iota(jnp.int32, (slot_rows, rows), 1)
        wanted = jnp.minimum(position + start, rows - 1)
        sel[pl.ds(group * slot_rows, slot_rows), :] = jnp.where(wanted == column, 1.0, 0.0).astype(
            jnp.bfloat16
        )
    for source in range(n_seq):
        length = jnp.int32(0)
        for j in range(n_seq):
            length = length + jnp.where(table_ref[source, j] == s, lengths_ref[source, j], 0)
        slot = lax.broadcasted_iota(jnp.int32, (1, slot_rows), 1)
        mask[source] = jnp.where(slot < length, 1.0, 0.0)

    finish_dec()
    normalise(dec_all.at[0], dec_normed, targets, dec_gain_ref, 0)
    for copy in weight_copies:
        copy.wait()
    project_queries(0)

    own_in.wait()
    for copy in in_copies:
        copy.wait()

    tile = min(256, units)

    def hidden_chunk(i, carry):
        cols = pl.ds(pl.multiple_of((i % (units // tile)) * tile, tile), tile)
        span = pl.ds(pl.multiple_of((i // (units // tile)) * chunk, chunk), chunk)
        acc = jnp.zeros((chunk, tile), jnp.float32)
        for k in range(n_seq):
            acc = acc + jnp.dot(
                normed[span, pl.ds(k * depth, depth)],
                win[k, :, cols],
                preferred_element_type=jnp.float32,
            )
        hidden[span, cols] = jnp.maximum(acc, 0.0).astype(jnp.bfloat16)
        return carry

    lax.fori_loop(0, (total_rows // chunk) * (units // tile), hidden_chunk, 0)

    def send_copy(slot, span):
        return pltpu.make_async_remote_copy(
            src_ref=part_out.at[slot, span],
            dst_ref=part_in.at[m, span],
            send_sem=red_ps.at[slot],
            recv_sem=red_pr.at[m],
            device_id=(s, slot),
            device_id_type=MESH,
        )

    def send_block(block, j):
        slot = block * per_block + j

        def rows_chunk(i, carry):
            span = pl.ds(pl.multiple_of(i * chunk, chunk), chunk)
            part_out[slot, span, :] = jnp.dot(
                hidden[span, :], wout[block, j], preferred_element_type=jnp.float32
            ).astype(jnp.bfloat16)

            @pl.when(slot != m)
            def _():
                send_copy(slot, span).start()

            return carry

        lax.fori_loop(0, total_rows // chunk, rows_chunk, 0)

    def receive_block(bits, j):
        peer = flip_any(bits)
        out_copy(bits, peer, j).wait()
        send_block(peer, j)

    inner = (s % 2 + s // 2) % 2

    def flip_any(bits):
        if isinstance(bits, int):
            return flip(s, bits)
        return flip(s, 2) * (3 - bits) + flip(s, 3) * (bits - 2)

    later = list(range(2, n_seq))
    if n_seq == 4:
        later = [2 + inner, 3 - inner]
    for j in range(per_block):
        own_out[j].wait()
        send_block(s, j)
    for j in range(per_block):
        receive_block(1, j)
    for j in range(per_block):
        for bits in later:
            receive_block(bits, j)

    everything = pl.ds(0, total_rows)
    for bits in range(1, n_mp):
        send_copy(flip(m, bits), everything).wait_send()
    for bits in range(1, n_mp):
        peer = flip(m, bits)
        pltpu.make_async_remote_copy(
            src_ref=part_out.at[peer],
            dst_ref=part_in.at[peer],
            send_sem=red_ps.at[peer],
            recv_sem=red_pr.at[peer],
            device_id=(s, peer),
            device_id_type=MESH,
        ).wait_recv()

    def reduce_rows(block):
        span = pl.ds(pl.multiple_of(block * rows, rows), rows)
        total = part_out[m, span, :].astype(jnp.float32)
        for bits in range(1, n_mp):
            total = total + part_in[flip(m, bits), span, :].astype(jnp.float32)
        return total

    red_z = []
    for bits in z_order(n_seq):
        peer = flip(s, bits)
        z_out[bits] = reduce_rows(peer).astype(jnp.bfloat16)
        copy = pltpu.make_async_remote_copy(
            src_ref=z_out.at[bits],
            dst_ref=z_in.at[bits],
            send_sem=red_zs.at[bits],
            recv_sem=red_zr.at[bits],
            device_id=(peer, m),
            device_id_type=MESH,
        )
        copy.start()
        red_z.append(copy)
    total = reduce_rows(s)
    for bits, copy in zip(z_order(n_seq), red_z):
        copy.wait()
        total = total + z_in[bits].astype(jnp.float32)
    enc_half[...] = (enc_ref[...].astype(jnp.float32) + total).astype(jnp.bfloat16)

    def select(group):
        span = pl.ds(pl.multiple_of(group * slot_rows, slot_rows), slot_rows)
        return jnp.dot(
            sel[span, :], enc_half[...], preferred_element_type=jnp.float32
        ).astype(jnp.bfloat16)

    my_slots = pl.ds(pl.multiple_of(s * slot_rows, slot_rows), slot_rows)
    slot_z = []
    for bits in z_order(n_seq):
        peer = flip(s, bits)
        slot_out[bits] = select(peer)
        copy = pltpu.make_async_remote_copy(
            src_ref=slot_out.at[bits],
            dst_ref=slots.at[m, my_slots],
            send_sem=slot_zs.at[bits],
            recv_sem=slot_zr.at[bits],
            device_id=(peer, m),
            device_id_type=MESH,
        )
        copy.start()
        slot_z.append(copy)
    slots[m, my_slots, :] = select(s)
    for copy in slot_z:
        copy.wait()

    plane_gather(slots, slot_ps, slot_pr)()
    normalise(slots, memory, n_seq * slot_rows, final_gain_ref, 0)
    project_memory(0)

    state = dec_ref[...].astype(jnp.float32)
    for layer in range(layers):
        if layer > 0:
            dec_all[layer, m] = state.astype(jnp.bfloat16)
            plane_gather(dec_all.at[layer], dec_ps.at[layer], dec_pr.at[layer])()
            normalise(dec_all.at[layer], dec_normed, targets, dec_gain_ref, layer)
            project_queries(layer)
        attend()
        scatter_output(layer)
        if layer + 1 < layers:
            project_memory(layer + 1)
        state = state + collect_output(layer)
    out_ref[...] = state.astype(out_ref.dtype)


def whole_fast(
    enc_rows,
    ffn_in,
    ffn_out,
    enc_gain,
    final_gain,
    sent_lengths,
    group_table,
    dec_rows,
    dec_gain,
    w_query,
    w_key,
    w_value,
    w_output,
):
    n_seq, n_mp = lax.axis_size("seq"), lax.axis_size("mp")
    rows, width = enc_rows.shape
    depth, units = ffn_in.shape[0], ffn_in.shape[1] // n_seq
    out_width = ffn_out.shape[1]
    total = rows * n_seq
    full = width * n_mp
    targets = dec_rows.shape[0]
    layers, _, heads_width = w_query.shape
    slot_total = 2 * rows
    per_block = out_width // width
    half = jnp.bfloat16
    dma = pltpu.SemaphoreType.DMA
    return pl.pallas_call(
        functools.partial(ffn_kernel, n_seq, n_mp),
        out_shape=jax.ShapeDtypeStruct(dec_rows.shape, dec_rows.dtype),
        in_specs=[pl.BlockSpec(memory_space=pltpu.VMEM)] * 3
        + [pl.BlockSpec(memory_space=pltpu.SMEM)] * 2
        + [pl.BlockSpec(memory_space=pltpu.VMEM)] * 2
        + [pl.BlockSpec(memory_space=pl.ANY)] * 6,
        out_specs=pl.BlockSpec(memory_space=pltpu.VMEM),
        scratch_shapes=[
            pltpu.VMEM((n_mp, total, width), jnp.bfloat16),
            pltpu.VMEM((total, full), jnp.bfloat16),
            pltpu.VMEM((n_seq, depth, units), jnp.bfloat16),
            pltpu.VMEM((n_seq, per_block, units, width), jnp.bfloat16),
            pltpu.VMEM((total, units), jnp.bfloat16),
            pltpu.VMEM((n_mp, total, width), jnp.bfloat16),
            pltpu.VMEM((n_mp, total, width), jnp.bfloat16),
            pltpu.VMEM((n_seq, rows, width), jnp.bfloat16),
            pltpu.VMEM((n_seq, rows, width), jnp.bfloat16),
            dma((n_seq,)),
            dma((n_seq,)),
            dma((n_mp,)),
            dma((n_mp,)),
            dma((n_seq,)),
            dma((n_seq,)),
            dma((n_seq, per_block)),
            dma((n_seq, per_block)),
            dma((n_mp,)),
            dma((n_mp,)),
            dma((n_seq,)),
            dma((n_seq,)),
            dma((4,)),
            pltpu.VMEM(w_query.shape, half),
            pltpu.VMEM(w_key.shape, half),
            pltpu.VMEM(w_value.shape, half),
            pltpu.VMEM(w_output.shape, half),
            dma((4,)),
            pltpu.VMEM((layers, n_mp, targets, width), half),
            pltpu.VMEM((targets, full), half),
            pltpu.VMEM((targets, heads_width), half),
            pltpu.VMEM((rows, width), half),
            pltpu.VMEM((n_seq, slot_total // n_seq, width), half),
            pltpu.VMEM((n_mp, slot_total, width), half),
            pltpu.VMEM((slot_total, full), half),
            pltpu.VMEM((slot_total, heads_width), half),
            pltpu.VMEM((slot_total, heads_width), half),
            pltpu.VMEM((targets, heads_width), half),
            pltpu.VMEM((layers, n_mp, targets, width), half),
            pltpu.VMEM((layers, n_mp, targets, width), half),
            dma((layers, n_mp)),
            dma((layers, n_mp)),
            dma((n_seq,)),
            dma((n_seq,)),
            dma((n_mp,)),
            dma((n_mp,)),
            dma((layers, n_mp)),
            dma((layers, n_mp)),
            pltpu.VMEM((slot_total, rows), half),
            pltpu.VMEM((n_seq, 1, slot_total // n_seq), jnp.float32),
            dma((per_block,)),
        ],
        compiler_params=pltpu.CompilerParams(
            collective_id=0, has_side_effects=True, vmem_limit_bytes=60 * 1024 * 1024
        ),
    )(
        enc_rows,
        enc_gain.reshape(1, full),
        final_gain.reshape(1, full),
        sent_lengths,
        group_table,
        dec_rows,
        dec_gain,
        ffn_in,
        ffn_out,
        w_query,
        w_key,
        w_value,
        w_output,
    )


def fast_shapes(enc_rows, ffn_in, ffn_out, dec_rows, w_query):
    n_seq, n_mp = lax.axis_size("seq"), lax.axis_size("mp")
    power = (n_seq & (n_seq - 1)) == 0 and (n_mp & (n_mp - 1)) == 0
    aligned = (
        enc_rows.shape[1] % 128 == 0
        and ffn_in.shape[0] % 128 == 0
        and (ffn_in.shape[1] // n_seq) % 256 == 0
        and ffn_out.shape[1] % enc_rows.shape[1] == 0
        and enc_rows.shape[0] % 256 == 0
        and dec_rows.shape[0] % 256 == 0
        and (2 * enc_rows.shape[0] // n_seq) % 128 == 0
        and w_query.shape[2] % 256 == 0
        and w_query.shape[1] % 256 == 0
    )
    return power and aligned


def shards(
    enc_rows,
    ffn_in,
    ffn_out,
    enc_gain,
    final_gain,
    sent_lengths,
    group_table,
    dec_rows,
    dec_gain,
    w_query,
    w_key,
    w_value,
    w_output,
):
    group_count = lax.axis_size("seq")
    my_group = lax.axis_index("seq")
    col_width = enc_rows.shape[1]
    col_start = lax.axis_index("mp") * col_width
    row_count = enc_rows.shape[0]
    max_length = 2 * row_count // group_count
    fast = fast_shapes(enc_rows, ffn_in, ffn_out, dec_rows, w_query)
    if not fast:
        whole_rows = lax.all_gather(enc_rows, "mp", axis=1, tiled=True)
        normed = rms_scale(whole_rows.astype(jnp.float32), enc_gain).astype(jnp.bfloat16)
        full_in = lax.all_gather(ffn_in, "seq", axis=0, tiled=True)
        inner = jnp.dot(normed, full_in, preferred_element_type=jnp.float32)
        hidden = jnp.maximum(inner, 0.0).astype(jnp.bfloat16)
        partial_out = jnp.dot(
            hidden,
            lax.all_gather(ffn_out, "seq", axis=1, tiled=True),
            preferred_element_type=jnp.float32,
        )
    my_lengths = lax.dynamic_index_in_dim(sent_lengths, my_group, 0, keepdims=False)
    my_targets = lax.dynamic_index_in_dim(group_table, my_group, 0, keepdims=False)
    my_starts = jnp.cumsum(my_lengths) - my_lengths
    group_ids = jnp.arange(group_count, dtype=jnp.int32)
    matches = my_targets[None, :] == group_ids[:, None]
    send_starts = jnp.sum(jnp.where(matches, my_starts[None, :], 0), axis=1)
    positions = jnp.arange(max_length, dtype=jnp.int32)
    row_index = jnp.minimum(send_starts[:, None] + positions[None, :], row_count - 1)
    recv_lengths = jnp.sum(jnp.where(group_table == my_group, sent_lengths, 0), axis=1)
    live_mask = positions[None, :] < recv_lengths[:, None]
    if fast:
        return whole_fast(
            enc_rows,
            ffn_in,
            ffn_out,
            enc_gain,
            final_gain,
            sent_lengths,
            group_table,
            dec_rows,
            dec_gain,
            w_query,
            w_key,
            w_value,
            w_output,
        )
    kv_width = w_key.shape[2]
    weight_list = []
    for layer_index in range(LAYERS):
        weight_list.append(w_key[layer_index])
        weight_list.append(w_value[layer_index])
    enc_share = lax.psum_scatter(partial_out, "mp", scatter_dimension=1, tiled=True)
    encoded = enc_rows.astype(jnp.float32) + enc_share
    squares = lax.psum(jnp.sum(encoded * encoded, axis=1), "mp")
    gain_part = lax.dynamic_slice_in_dim(final_gain, col_start, col_width, 0)
    memory = (encoded * lax.rsqrt(squares / D + epsilon)[:, None] * gain_part).astype(jnp.bfloat16)
    blocks = memory[row_index]
    gathered = lax.all_gather(
        lax.all_to_all(blocks, "seq", split_axis=0, concat_axis=0, tiled=True),
        "mp",
        axis=2,
        tiled=True,
    )
    projected = tuple(
        (
            jnp.einsum(
                "std,de->ste", gathered, weight_matrix, preferred_element_type=jnp.float32
            ).astype(jnp.bfloat16)
            for weight_matrix in weight_list
        )
    )
    tgt_rows = dec_rows.shape[0]
    per_sentence = tgt_rows // group_count
    local_heads = kv_width // DH
    final_state = dec_rows.astype(jnp.float32)
    for layer_index in range(LAYERS):
        state_half = lax.all_gather(final_state.astype(jnp.bfloat16), "mp", axis=1, tiled=True)
        normed_rows = rms_scale(state_half.astype(jnp.float32), dec_gain[layer_index]).astype(
            jnp.bfloat16
        )
        queries = (
            jnp.dot(normed_rows, w_query[layer_index], preferred_element_type=jnp.float32)
            * DH ** (-0.5)
        ).astype(jnp.bfloat16)
        query_heads = queries.reshape(group_count, per_sentence, local_heads, DH)
        key_heads = projected[2 * layer_index].reshape(group_count, max_length, local_heads, DH)
        value_heads = projected[2 * layer_index + 1].reshape(
            group_count, max_length, local_heads, DH
        )
        scores = jnp.einsum(
            "sqhd,sthd->shqt", query_heads, key_heads, preferred_element_type=jnp.float32
        )
        scores = jnp.where(live_mask[:, None, None, :], scores, -jnp.inf)
        weights = jax.nn.softmax(scores, axis=-1).astype(jnp.bfloat16)
        attended = jnp.einsum(
            "shqt,sthd->sqhd", weights, value_heads, preferred_element_type=jnp.float32
        ).astype(jnp.bfloat16)
        final_state = final_state + lax.psum_scatter(
            jnp.dot(
                attended.reshape(tgt_rows, kv_width),
                w_output[layer_index],
                preferred_element_type=jnp.float32,
            ).astype(jnp.bfloat16),
            "mp",
            scatter_dimension=1,
            tiled=True,
        ).astype(jnp.float32)
    return final_state.astype(jnp.bfloat16)


def solution(mesh):
    in_specs = (
        P("seq", "mp"),
        P("seq", "mp"),
        P("mp", "seq"),
        P(),
        P(),
        P(),
        P(),
        P("seq", "mp"),
        P(),
        P(None, None, "mp"),
        P(None, None, "mp"),
        P(None, None, "mp"),
        P(None, "mp", None),
    )
    out_specs = P("seq", "mp")
    return jax.shard_map(shards, mesh=mesh, in_specs=in_specs, out_specs=out_specs, check_vma=False)
```
